32 devices in a mesh: field: 4 (over z), vrow: 2 (over core), vcol: 4 (over y, x).
Axes of the slice: x: 2, y: 2, z: 4, core: 2. Of those that a mesh axis runs over, the one named last changes fastest.
Arguments:
- blocks: bfloat16 [1024, 24, 2, 256], P(('vrow', 'vcol'), 'field'), may hold values from 0 to 1
- block_ids: int32 [8, 4, 6], P(('vrow', 'vcol'), 'field'), may hold values from 0 to 11, as said below
- block_counts: int32 [8, 4], P(('vrow', 'vcol'), 'field'), may hold values from 1 to 6, as said below
Outputs:
- tables: float32 [1024, 2, 2, 4, 2, 128], P(('vrow', 'field'), None, None, 'vcol')
The draws below stay inside these ranges and needn't reach their ends.
Inputs may be any that keep to these rules, and one draw needn't show every extreme that they name: `block_ids`: within each row of the last dimension the entries are distinct. `block_counts`: 6 is reached in every draw.
All inputs are finite; a program needn't handle non-finite values.
Results may differ from the reference program's by a relative error of at most 0.0003.
Values may be sent and summed in bfloat16 or wider, within the bound.
A program may use at most 64 MiB of HBM per device.

```python
import jax
import jax.numpy as jnp
from jax import lax

VS = 128
SBLK = 12
BLOCK = 256
OCC = 6
NSH = 8
V = 1024
NSAMP = 12288
N_FIELD = 4
N_VROW = 2
N_VCOL = 4


def draw_block_ids(key, part):
    keys = jax.random.split(jax.random.fold_in(key, 11), NSH * N_FIELD)
    picks = jax.vmap(lambda k: jax.random.permutation(k, SBLK)[:OCC])(keys)
    return picks.reshape(NSH, N_FIELD, OCC).astype(jnp.int32)


def draw_block_counts(key, part):
    first = jax.random.fold_in(key, 23)
    values = jax.random.randint(first, (NSH * N_FIELD,), 1, OCC + 1)
    where = jax.random.randint(jax.random.fold_in(key, 29), (), 0, NSH * N_FIELD)
    values = values.at[where].set(OCC)
    return values.reshape(NSH, N_FIELD).astype(jnp.int32)


def block_levels(own_key, dims, shards, smallest, top_value):
    def one(axis_at, parts):
        heights = jax.random.uniform(jax.random.fold_in(jax.random.fold_in(own_key, 6), axis_at), (parts,), jnp.float32, smallest / len(shards), top_value / len(shards))
        return jnp.repeat(jnp.exp(heights), dims[axis_at] // parts).reshape((-1,) + (1,) * (len(dims) - axis_at - 1))

    gain = one(*shards[0])
    for cut in shards[1:]:
        gain = gain * one(*cut)
    return gain


def setup_inputs(seed: int = 0) -> dict:
    key_of = jax.random.split(jax.random.key(seed), 4)
    return {
        "blocks": jnp.clip(1.0 * jax.random.uniform(key_of[0], (V, N_FIELD * OCC, 2, BLOCK), jnp.float32) ** block_levels(key_of[0], (V, N_FIELD * OCC, 2, BLOCK), ((0, 8), (1, 4)), -0.2, 0.2), 0.0, 1.0).astype(jnp.bfloat16),
        "block_ids": draw_block_ids(jax.random.fold_in(key_of[3], 71), 0),
        "block_counts": draw_block_counts(jax.random.fold_in(key_of[3], 71), 0),
    }


def reference(blocks, block_ids, block_counts):
    occ = block_ids.shape[-1]
    shaped = blocks.reshape(NSH, VS, N_FIELD, occ, 2, BLOCK).astype(jnp.float32)
    slots = jnp.arange(occ, dtype=jnp.int32)
    live = slots[None, None, :] < block_counts[:, :, None]
    onehot = (block_ids[:, :, :, None] == jnp.arange(SBLK, dtype=jnp.int32)[None, None, None, :]) & live[..., None]
    dense = jnp.einsum('sfok,svfocx->svcfkx', onehot.astype(jnp.float32), shaped, precision=lax.Precision.HIGHEST)
    dense = dense.astype(jnp.bfloat16).reshape(NSH * VS * 2, N_FIELD * SBLK * BLOCK).astype(jnp.float32)
    prods = jnp.dot(dense, dense.T, precision=lax.Precision.HIGHEST)
    prods = prods / NSAMP
    prods = prods.reshape(NSH * VS, 2, N_VROW, N_VCOL, VS, 2)
    return jnp.transpose(prods, (0, 1, 2, 3, 5, 4))
```

```python
import functools

import jax
import jax.numpy as jnp
from jax import lax
from jax.experimental import pallas as pl
from jax.experimental.pallas import tpu as pltpu
from jax.sharding import PartitionSpec as P

SBLK = 12
BLOCK = 256
MAX_PIECES = 4
STEPS_AHEAD = 2
AHEAD = 3
PLAN = (
    "S0", "S1", "o0", "X0", "Y0", "S2", "o1", "X1", "Y1", "S3",
    "s0", "o2", "X2", "s1", "Y2", "x0", "f0", "D0", "y0", "o3",
    "X3", "s2", "Y3", "x1", "f1", "D1", "y1", "f2", "D2", "s3",
    "f3", "D3", "x2", "y2", "d0", "t0", "x3", "y3", "d1", "t1",
    "d2", "d3",
)
LEVELS = 65535.0
HALF = 32768
MESH = pl.DeviceIdType.MESH


def partner(q, d, n):
    if n == 4:
        return (q + 1 - 2 * lax.rem(q, 2), lax.rem(q + 2, 4), 3 - q)[d - 1]
    return lax.rem(q + d, n)


def any_kernel(
    dims, scale, data, ids, counts, out, meta, rows, raw_cols, cols, part, code, tops, got, got_tops, mine_sum, rmeta, cmeta, rids, cids,
    row_local, meta_local,
    row_send, row_recv, col_send, col_recv, rm_send, rm_recv, cm_send, cm_recv,
    part_send, part_recv, top_send, top_recv,
):
    n_field, n_vrow, n_vcol, pieces, occ, width, per_chunk = dims
    f, r, q = lax.axis_index("field"), lax.axis_index("vrow"), lax.axis_index("vcol")
    relay = n_vcol == 4

    barrier = pltpu.get_barrier_semaphore()
    for d in range(1, n_vcol):
        pl.semaphore_signal(barrier, inc=1, device_id={"vcol": partner(q, d, n_vcol)}, device_id_type=MESH)
    for d in range(1, n_vrow):
        pl.semaphore_signal(barrier, inc=1, device_id={"vrow": lax.rem(r + d, n_vrow)}, device_id_type=MESH)
    for d in range(1, n_field):
        pl.semaphore_signal(barrier, inc=1, device_id={"field": lax.rem(f + d, n_field)}, device_id_type=MESH)

    meta[...] = jnp.full_like(meta, -1)
    slots = lax.broadcasted_iota(jnp.int32, (1, occ), 1)
    meta[:, 0:occ] = jnp.where(slots < counts[...], ids[0], -1)
    own = pltpu.make_async_copy(data, rows.at[0], row_local.at[0])
    own.start()
    for v in range(n_vrow):
        cols[v, occ] = jnp.zeros_like(cols[v, occ])

    pl.semaphore_wait(barrier, n_vcol + n_vrow + n_field - 3)

    own_r = pltpu.make_async_copy(meta, rids.at[0], meta_local.at[0])
    own_r.start()
    own_c = pltpu.make_async_copy(meta, cids.at[0], meta_local.at[1])
    own_c.start()

    def span(p):
        return pl.ds(p * width, width)

    sends = []

    def send(src, dst, s, w, where):
        c = pltpu.make_async_remote_copy(
            src_ref=src, dst_ref=dst, send_sem=s, recv_sem=w, device_id=where, device_id_type=MESH
        )
        c.start()
        sends.append(c)
        return c

    row_meta, col_meta, row_copy, col_copy = {}, {}, {}, {}

    def send_rows(p):
        for d in range(1, 3 if relay else n_vcol):
            to = {"vcol": partner(q, d, n_vcol)}
            row_copy[d, p] = send(data.at[span(p)], rows.at[d, span(p)], row_send.at[d, p], row_recv.at[d, p], to)

    for d in range(1, n_vrow):
        to = {"vrow": lax.rem(r + d, n_vrow)}
        col_meta[d] = send(meta, cmeta.at[d], cm_send.at[d], cm_recv.at[d], to)
    for d in range(1, n_vcol):
        to = {"vcol": partner(q, d, n_vcol)}
        row_meta[d] = send(meta, rmeta.at[d], rm_send.at[d], rm_recv.at[d], to)
    for p in range(pieces):
        for d in range(1, n_vrow):
            to = {"vrow": lax.rem(r + d, n_vrow)}
            col_copy[d, p] = send(
                data.at[span(p)],
                raw_cols.at[d, span(p)],
                col_send.at[d, p], col_recv.at[d, p], to,
            )
        if p < (STEPS_AHEAD if relay else pieces):
            send_rows(p)

    own.wait()
    own_r.wait()
    own_c.wait()
    for d in range(1, n_vrow):
        col_meta[d].wait_recv()
        c = pltpu.make_async_copy(cmeta.at[d], cids.at[d], meta_local.at[1])
        c.start()
        c.wait()
    for d in range(1, n_vrow):
        for p in range(pieces):
            col_copy[d, p].wait_recv()
    ch, vs = rows.shape[3], rows.shape[1]
    n = ch * vs
    to_row = lax.broadcasted_iota(jnp.int32, (n, n), 0)
    from_row = lax.broadcasted_iota(jnp.int32, (n, n), 1)
    order = jnp.where(from_row == lax.rem(to_row, vs) * ch + to_row // vs, 1.0, 0.0).astype(jnp.bfloat16)
    for v in range(n_vrow):
        for o in range(occ):
            block = (raw_cols[v, :, o] if v else rows[0, :, o]).reshape(n, rows.shape[-1])
            turned = jnp.dot(order, block, preferred_element_type=jnp.float32)
            cols[v, o] = turned.astype(jnp.bfloat16)

    match = {}
    part_sends = []

    def matches(d):
        if d:
            row_meta[d].wait_recv()
            c = pltpu.make_async_copy(rmeta.at[d], rids.at[d], meta_local.at[0])
            c.start()
            c.wait()
        theirs = [[cids[v, 0, o] for o in range(occ)] for v in range(n_vrow)]
        found = []
        for o in range(occ):
            mine = rids[d, 0, o]
            for v in range(n_vrow):
                m = jnp.int32(occ)
                for k in range(occ):
                    m = jnp.where((mine >= 0) & (mine == theirs[v][k]), jnp.int32(k), m)
                found.append(m)
        return found

    def compute(d, p):
        if d not in match:
            match[d] = matches(d)
        for v in range(n_vrow):
            acc = None
            for o in range(occ):
                lhs = rows[d, p * width : (p + 1) * width, o].reshape(ch * width, rows.shape[-1])
                rhs = cols[v, match[d][o * n_vrow + v]]
                t = lax.dot_general(lhs, rhs, (((1,), (1,)), ((), ())), preferred_element_type=jnp.float32)
                acc = t if acc is None else acc + t
            n = acc.shape[1]
            at = pl.multiple_of(lax.rem(r + v, n_vrow) * n, n)
            part[d, p, :, pl.ds(at, n)] = acc
            top = jnp.max(acc, axis=0, keepdims=True)
            inverse = jnp.where(top > 0, 1.0 / top, 0.0)
            level = ((acc * inverse) * LEVELS + 0.5).astype(jnp.int32) - HALF
            code[d, p, :, pl.ds(at, n)] = level.astype(jnp.int16)
            tops[d, p, :, pl.ds(at, n)] = top
        s = q if d == 0 else partner(q, d, n_vcol)
        g = s * pieces + p
        dest = g // per_chunk
        place = g - dest * per_chunk
        to = {"field": dest}
        c = pltpu.make_async_remote_copy(
            src_ref=code.at[d, p], dst_ref=got.at[f, place],
            send_sem=part_send.at[d, p], recv_sem=part_recv.at[f, place],
            device_id=to, device_id_type=MESH,
        )
        t = pltpu.make_async_remote_copy(
            src_ref=tops.at[d, p], dst_ref=got_tops.at[f, place],
            send_sem=top_send.at[d, p], recv_sem=top_recv.at[f, place],
            device_id=to, device_id_type=MESH,
        )

        @pl.when(dest != f)
        def _():
            t.start()
            c.start()

        @pl.when(dest == f)
        def _():
            mine_sum[place] = part[d, p]

        part_sends.append((dest, c, t))

    def forward(p):
        first = pl.ds(p * width, width // 2)
        second = pl.ds(p * width + width // 2, width - width // 2)
        row_copy[1, p].wait_recv()
        a = send(rows.at[1, first], rows.at[3, first],
                 row_send.at[3, p], row_recv.at[3, p], {"vcol": partner(q, 2, 4)})
        row_copy[2, p].wait_recv()
        b = send(rows.at[2, second], rows.at[3, second],
                 row_send.at[0, p], row_recv.at[0, p], {"vcol": partner(q, 1, 4)})
        row_copy[3, p] = (a, b)
        if p + STEPS_AHEAD < pieces:
            send_rows(p + STEPS_AHEAD)

    compute(0, 0)
    for p in range(pieces):
        if relay:
            forward(p)
        for d in range(1, 3 if relay else n_vcol):
            if not relay:
                row_copy[d, p].wait_recv()
            compute(d, p)
        if p + 1 < pieces:
            compute(0, p + 1)
        if relay and p:
            for c in row_copy[3, p - 1]:
                c.wait_recv()
            compute(3, p - 1)
    if relay:
        for c in row_copy[3, pieces - 1]:
            c.wait_recv()
        compute(3, pieces - 1)

    for place in range(per_chunk):
        total = mine_sum[place]
        for d in range(1, n_field):
            src = lax.rem(f + d, n_field)
            for buf, land, gone, came in (
                (code, got, part_send, part_recv), (tops, got_tops, top_send, top_recv),
            ):
                pltpu.make_async_remote_copy(
                    src_ref=buf.at[0, 0], dst_ref=land.at[src, place],
                    send_sem=gone.at[0, 0], recv_sem=came.at[src, place],
                    device_id={"field": src}, device_id_type=MESH,
                ).wait_recv()
            level = (got[src, place].astype(jnp.int32) + HALF).astype(jnp.float32)
            total = total + level * (got_tops[src, place] * (1.0 / LEVELS))
        parts = n_vrow * ch
        for k in range(parts):
            out[pl.ds(place * ch * width * parts + k, ch * width, parts), :] = total[:, k * vs : (k + 1) * vs]
    for c in sends:
        c.wait_send()
    for dest, c, t in part_sends:
        @pl.when(dest != f)
        def _():
            c.wait_send()
            t.wait_send()


def on_any_device(blocks, block_ids, block_counts):
    n_field, n_vrow, n_vcol = (lax.axis_size(a) for a in ("field", "vrow", "vcol"))
    vs, occ, ch, x = blocks.shape
    chunk = n_vcol * vs // n_field
    width = min(vs // MAX_PIECES, chunk)
    pieces = vs // width
    per_chunk = chunk // width
    data = blocks
    c = ch * vs
    wide = n_vrow * c
    dims = (n_field, n_vrow, n_vcol, pieces, occ, width, per_chunk)
    dma = pltpu.SemaphoreType.DMA
    scale = 1.0 / (n_field * SBLK * BLOCK)
    out = pl.pallas_call(
        functools.partial(any_kernel, dims, scale),
        out_shape=jax.ShapeDtypeStruct((chunk * ch * n_vrow * ch, vs), jnp.float32),
        in_specs=[pl.BlockSpec(memory_space=pl.ANY)] + [pl.BlockSpec(memory_space=pltpu.VMEM)] * 2,
        out_specs=pl.BlockSpec(memory_space=pltpu.VMEM),
        scratch_shapes=[
            pltpu.VMEM((1, 128), jnp.int32),
            pltpu.VMEM((n_vcol, vs, occ, ch, x), jnp.bfloat16),
            pltpu.VMEM((n_vrow, vs, occ, ch, x), jnp.bfloat16),
            pltpu.VMEM((n_vrow, occ + 1, ch * vs, x), jnp.bfloat16),
            pltpu.VMEM((n_vcol, pieces, ch * width, wide), jnp.float32),
            pltpu.VMEM((n_vcol, pieces, ch * width, wide), jnp.int16),
            pltpu.VMEM((n_vcol, pieces, 1, wide), jnp.float32),
            pltpu.VMEM((n_field, per_chunk, ch * width, wide), jnp.int16),
            pltpu.VMEM((n_field, per_chunk, 1, wide), jnp.float32),
            pltpu.VMEM((per_chunk, ch * width, wide), jnp.float32),
            pltpu.VMEM((n_vcol, 1, 128), jnp.int32),
            pltpu.VMEM((n_vrow, 1, 128), jnp.int32),
            pltpu.SMEM((n_vcol, 1, 128), jnp.int32),
            pltpu.SMEM((n_vrow, 1, 128), jnp.int32),
            dma((1,)),
            dma((2,)),
            dma((n_vcol, pieces)),
            dma((n_vcol, pieces)),
            dma((n_vrow, pieces)),
            dma((n_vrow, pieces)),
            dma((n_vcol,)),
            dma((n_vcol,)),
            dma((n_vrow,)),
            dma((n_vrow,)),
            dma((n_vcol, pieces)),
            dma((n_field, per_chunk)),
            dma((n_vcol, pieces)),
            dma((n_field, per_chunk)),
        ],
        compiler_params=pltpu.CompilerParams(collective_id=1, has_side_effects=True),
    )(data, block_ids, block_counts)
    return (out * scale).reshape(chunk, ch, n_vrow, 1, ch, vs)


def square_kernel(
    dims, data, ids, counts, out,
    meta, raw, cols, rows, mine, hold, code, tops, got, got_tops, code2, tops2, got2, got2_tops, turn, turn_tops, turned, turned_tops,
    rmeta, cmeta, rids, cids,
    raw_sem, meta_local, col_sem, own_send, own_recv, far_send, far_recv,
    m_send, m_recv, part_send, part_recv, top_send, top_recv, part2_send, part2_recv, top2_send, top2_recv,
    turn_send, turn_recv, ttop_send, ttop_recv, two,
):
    n_field, n_vrow, n_vcol, groups, occ, vs, ch = dims
    n, half = cols.shape[3], cols.shape[4]
    gw = n // groups
    f, r, q = lax.axis_index("field"), lax.axis_index("vrow"), lax.axis_index("vcol")
    beside, across = f + 1 - 2 * lax.rem(f, 2), lax.rem(f + 2, n_field)
    over = [q, partner(q, 1, 4), partner(q, 2, 4), partner(q, 3, 4)]
    twin = {"vrow": 1 - r}
    near = {1: {"vcol": over[1]}, 2: {"vcol": over[2]}}
    odd = lax.rem(q // 2 + q, 2)
    place = [1 - odd, odd]

    barrier = pltpu.get_barrier_semaphore()
    for to in (twin, near[1], near[2]):
        pl.semaphore_signal(barrier, inc=1, device_id=to, device_id_type=MESH)

    @pl.when(f + 1 < n_field)
    def _():
        pl.semaphore_signal(barrier, inc=1, device_id={"field": lax.rem(f + 1, n_field)}, device_id_type=MESH)

    @pl.when(f > 0)
    def _():
        pl.semaphore_signal(barrier, inc=1, device_id={"field": lax.rem(f + n_field - 1, n_field)}, device_id_type=MESH)

    loads = []
    for o in range(occ):
        c = pltpu.make_async_copy(data.at[:, o], raw.at[o], raw_sem.at[o])
        c.start()
        loads.append(c)
    meta[...] = jnp.full_like(meta, -1)
    slots = lax.broadcasted_iota(jnp.int32, (1, occ), 1)
    meta[:, 0:occ] = jnp.where(slots < counts[...], ids[0], -1)
    own_r = pltpu.make_async_copy(meta, rids.at[0], meta_local.at[0])
    own_r.start()
    own_c = pltpu.make_async_copy(meta, cids.at[0], meta_local.at[1])
    own_c.start()
    for b in range(2):
        for v in range(n_vrow):
            cols[b, v, occ] = jnp.zeros_like(cols[b, v, occ])
    to_row = lax.broadcasted_iota(jnp.int32, (n, n), 0)
    from_row = lax.broadcasted_iota(jnp.int32, (n, n), 1)
    order = jnp.where(from_row == lax.rem(to_row, vs) * ch + to_row // vs, 1.0, 0.0).astype(jnp.bfloat16)
    for o in range(occ):
        loads[o].wait()
        sorted_rows = jnp.dot(order, raw[o].reshape(n, 2 * half), preferred_element_type=jnp.float32)
        for b in range(2):
            cols[place[b], 0, o] = sorted_rows[:, b * half : (b + 1) * half].astype(jnp.bfloat16)
    own_r.wait()
    own_c.wait()

    @pl.when((f > 0) & (f + 1 < n_field))
    def _():
        pl.semaphore_wait(barrier, 5)

    @pl.when((f == 0) | (f + 1 == n_field))
    def _():
        pl.semaphore_wait(barrier, 4)

    sends = []

    def send(src, dst, s, t, where):
        c = pltpu.make_async_remote_copy(
            src_ref=src, dst_ref=dst, send_sem=s, recv_sem=t, device_id=where, device_id_type=MESH
        )
        c.start()
        sends.append(c)
        return c

    up, down = {"field": lax.rem(f + 1, n_field)}, {"field": lax.rem(f + n_field - 1, n_field)}

    @pl.when((f > 0) & (f + 1 < n_field))
    def _():
        pl.semaphore_signal(two.at[0], inc=1, device_id=up, device_id_type=MESH)
        pl.semaphore_signal(two.at[1], inc=1, device_id=down, device_id_type=MESH)

    live = pl.ds(0, occ)
    twin_copy = send(cols.at[:, 0, live], cols.at[:, 1, live], col_sem.at[0], col_sem.at[1], twin)
    c_meta = send(meta, cmeta.at[0], m_send.at[0], m_recv.at[0], twin)
    r_meta = {}
    for d in (1, 2):
        r_meta[d] = send(meta, rmeta.at[d], m_send.at[d], m_recv.at[d], near[d])
    own_copy, far_copy = {}, {}

    def span(g):
        return pl.ds(g * gw, gw)

    def send_own(g):
        for d in (1, 2):
            own_copy[d, g] = send(
                cols.at[2 - d, 0, live, span(g)], rows.at[d - 1, :, span(g)], own_send.at[d, g], own_recv.at[d, g], near[d]
            )

    def send_far(g):
        for d in (1, 2):
            far_copy[3 - d, g] = send(
                rows.at[d - 1, :, span(g)], rows.at[4 - d, :, span(g)], far_send.at[3 - d, g], far_recv.at[3 - d, g],
                near[3 - d],
            )

    for g in range(min(AHEAD, groups)):
        send_own(g)

    @pl.when(f < 2)
    def _():
        pl.semaphore_wait(two.at[1], 1)

    @pl.when(f >= 2)
    def _():
        pl.semaphore_wait(two.at[0], 1)

    c_meta.wait_recv()
    c = pltpu.make_async_copy(cmeta.at[0], cids.at[1], meta_local.at[1])
    c.start()
    c.wait()
    theirs = [[cids[v, 0, o] for o in range(occ)] for v in range(n_vrow)]

    def matches(d):
        if d:
            if d > 1:
                r_meta[d].wait_recv()
            c = pltpu.make_async_copy(rmeta.at[d], rids.at[d], meta_local.at[0])
            c.start()
            c.wait()
        found = {}
        for o in range(occ):
            own = rids[d, 0, o]
            for v in range(n_vrow):
                m = jnp.int32(occ)
                for k in range(occ):
                    m = jnp.where((own >= 0) & (own == theirs[v][k]), jnp.int32(k), m)
                found[o, v] = m
        return found

    match = {}
    part_sends = []

    def encode(acc):
        top = jnp.max(acc, axis=0, keepdims=True)
        inverse = jnp.where(top > 0, 1.0 / top, 0.0)
        level = ((acc * inverse) * LEVELS + 0.5).astype(jnp.int32) - HALF
        return level.astype(jnp.int16), top

    def decode(level, top):
        return (level.astype(jnp.int32) + HALF).astype(jnp.float32) * (top * (1.0 / LEVELS))

    def first_hop(dest, d, g):
        i = jnp.where(dest == beside, 0, 1)
        to = {"field": beside}
        return (
            pltpu.make_async_remote_copy(
                src_ref=code.at[d, g], dst_ref=got.at[i, g],
                send_sem=part_send.at[d, g], recv_sem=part_recv.at[i, g], device_id=to, device_id_type=MESH,
            ),
            pltpu.make_async_remote_copy(
                src_ref=tops.at[d, g], dst_ref=got_tops.at[i, g],
                send_sem=top_send.at[d, g], recv_sem=top_recv.at[i, g], device_id=to, device_id_type=MESH,
            ),
        )

    def came(i, g):
        for c in (
            pltpu.make_async_remote_copy(
                src_ref=code.at[0, g], dst_ref=got.at[i, g], send_sem=part_send.at[0, g], recv_sem=part_recv.at[i, g],
                device_id={"field": beside}, device_id_type=MESH,
            ),
            pltpu.make_async_remote_copy(
                src_ref=tops.at[0, g], dst_ref=got_tops.at[i, g], send_sem=top_send.at[0, g], recv_sem=top_recv.at[i, g],
                device_id={"field": beside}, device_id_type=MESH,
            ),
        ):
            c.wait_recv()
        return decode(got[i, g], got_tops[i, g])

    second_hop = []
    for g in range(groups):
        to = {"field": across}
        second_hop.append((
            pltpu.make_async_remote_copy(
                src_ref=code2.at[g], dst_ref=got2.at[g], send_sem=part2_send.at[g], recv_sem=part2_recv.at[g],
                device_id=to, device_id_type=MESH,
            ),
            pltpu.make_async_remote_copy(
                src_ref=tops2.at[g], dst_ref=got2_tops.at[g], send_sem=top2_send.at[g], recv_sem=top2_recv.at[g],
                device_id=to, device_id_type=MESH,
            ),
        ))

    def merge(d, g):
        @pl.when(over[d] == f)
        def _():
            mine[g] += came(0, g)

        @pl.when(over[d] == across)
        def _():
            code2[g], tops2[g] = encode(hold[g] + came(1, g))
            for c in reversed(second_hop[g]):
                c.start()

    def summed(g):
        for c in second_hop[g]:
            c.wait_recv()
        return mine[g] + decode(got2[g], got2_tops[g])

    def compute(d, g):
        if d not in match:
            match[d] = matches(d)
        at = pl.ds(g * gw, gw)
        halves = []
        for v in range(n_vrow):
            acc = None
            for o in range(occ):
                k = match[d][o, v]
                if d in (1, 2):
                    lhs, rhs = rows[d - 1, o, at], cols[d - 1, v, k]
                else:
                    lhs = [cols[b, 0, o, at] if d == 0 else rows[2 + b, o, at] for b in range(2)]
                    lhs = jnp.concatenate(lhs, axis=1)
                    rhs = jnp.concatenate([cols[b, v, k] for b in range(2)], axis=1)
                t = lax.dot_general(lhs, rhs, (((1,), (1,)), ((), ())), preferred_element_type=jnp.float32)
                acc = t if acc is None else acc + t
            halves.append(acc)
        dest = over[d]

        stays = lax.rem(dest, 2) == lax.rem(f, 2)
        c, t = first_hop(dest, d, g)

        def at(v):
            return pl.ds(pl.multiple_of(lax.rem(r + v, n_vrow) * n, n), n)

        @pl.when(dest == f)
        def _():
            for v in range(n_vrow):
                mine[g, :, at(v)] = halves[v]

        @pl.when(dest == across)
        def _():
            for v in range(n_vrow):
                hold[g, :, at(v)] = halves[v]

        @pl.when(jnp.logical_not(stays))
        def _():
            for v in range(n_vrow):
                code[d, g, :, at(v)], tops[d, g, :, at(v)] = encode(halves[v])
            t.start()
            c.start()

        part_sends.append((jnp.logical_not(stays), c, t))

    swaps = (f == over[1]) | (f == over[2])
    turn_copies = {}

    def swap(a):
        rows_of = range(a * groups // ch, (a + 1) * groups // ch)
        for b in range(n_vrow):
            to = {"field": q, "vrow": b, "vcol": f}
            turn_copies[a, b] = (
                pltpu.make_async_remote_copy(
                    src_ref=turn.at[a, b], dst_ref=turned.at[r, a],
                    send_sem=turn_send.at[a, b], recv_sem=turn_recv.at[r, a],
                    device_id=to, device_id_type=MESH,
                ),
                pltpu.make_async_remote_copy(
                    src_ref=turn_tops.at[a, b], dst_ref=turned_tops.at[r, a],
                    send_sem=ttop_send.at[a, b], recv_sem=ttop_recv.at[r, a],
                    device_id=to, device_id_type=MESH,
                ),
            )

        @pl.when(swaps)
        def _():
            for g in rows_of:
                mine[g] = summed(g)
            for b in range(n_vrow):
                each = [mine[g, :, b * n : (b + 1) * n] for g in rows_of]
                turn[a, b], turn_tops[a, b] = encode(jnp.concatenate(each, axis=0))
                for c in reversed(turn_copies[a, b]):
                    c.start()

    def step(kind, i):
        if kind in "SXYD":
            compute("SXYD".index(kind), i)
        elif kind in "sxyd":
            merge("sxyd".index(kind), i)
        elif kind == "o":
            for d in (1, 2):
                own_copy[d, i].wait_recv()
            if i == 0:
                r_meta[1].wait_recv()
                r_meta[3] = send(rmeta.at[1], rmeta.at[3], m_send.at[3], m_recv.at[3], near[2])
            send_far(i)
            if i + AHEAD < groups:
                send_own(i + AHEAD)
        elif kind == "f":
            for d in (1, 2):
                far_copy[d, i].wait_recv()
        else:
            swap(i)

    twin_copy.wait_recv()
    for name in PLAN:
        step(name[0], int(name[1:]))

    parts = n_vrow * ch

    def put(a, k, values):
        out[pl.ds(a * parts + k, vs, ch * parts), :] = values

    def held(a, k):
        each = [mine[g, :, k * vs : (k + 1) * vs] for g in range(a * groups // ch, (a + 1) * groups // ch)]
        return jnp.concatenate(each, axis=0)

    @pl.when(jnp.logical_not(swaps))
    def _():
        for a in range(ch):
            for g in range(a * groups // ch, (a + 1) * groups // ch):
                total = summed(g)
                at = (g * gw) % vs
                for k in range(parts):
                    out[pl.ds((at * ch + a) * parts + k, gw, ch * parts), :] = total[:, k * vs : (k + 1) * vs]

    @pl.when(swaps)
    def _():
        for b in range(ch):
            for v in range(n_vrow):
                for land, came, gone, buf in (
                    (turned, turn_recv, turn_send, turn), (turned_tops, ttop_recv, ttop_send, turn_tops),
                ):
                    pltpu.make_async_remote_copy(
                        src_ref=buf.at[0, 0], dst_ref=land.at[v, b],
                        send_sem=gone.at[0, 0], recv_sem=came.at[v, b],
                        device_id={"field": q, "vrow": r, "vcol": f}, device_id_type=MESH,
                    ).wait_recv()
                back = jnp.transpose(decode(turned[v, b], turned_tops[v, b]))
                k = v * ch + b
                for a in range(ch):
                    put(a, k, held(a, k) + back[a * vs : (a + 1) * vs])
        for c, t in turn_copies.values():
            c.wait_send()
            t.wait_send()

    for c in sends:
        c.wait_send()
    for sent, c, t in part_sends:
        @pl.when(sent)
        def _():
            c.wait_send()
            t.wait_send()
    for c, t in second_hop:
        c.wait_send()
        t.wait_send()


def on_square_device(blocks, block_ids, block_counts):
    n_field, n_vrow, n_vcol = (lax.axis_size(a) for a in ("field", "vrow", "vcol"))
    vs, occ, ch, x = blocks.shape
    n = ch * vs
    groups = 4
    gw = n // groups
    half = x // 2
    dims = (n_field, n_vrow, n_vcol, groups, occ, vs, ch)
    dma = pltpu.SemaphoreType.DMA
    wide = n_vrow * n
    out = pl.pallas_call(
        functools.partial(square_kernel, dims),
        out_shape=jax.ShapeDtypeStruct((vs * ch * n_vrow * ch, vs), jnp.float32),
        in_specs=[pl.BlockSpec(memory_space=pl.ANY)] + [pl.BlockSpec(memory_space=pltpu.VMEM)] * 2,
        out_specs=pl.BlockSpec(memory_space=pltpu.VMEM),
        scratch_shapes=[
            pltpu.VMEM((1, 128), jnp.int32),
            pltpu.VMEM((occ, vs, ch, x), jnp.bfloat16),
            pltpu.VMEM((2, n_vrow, occ + 1, n, half), jnp.bfloat16),
            pltpu.VMEM((4, occ, n, half), jnp.bfloat16),
            pltpu.VMEM((groups, gw, wide), jnp.float32),
            pltpu.VMEM((groups, gw, wide), jnp.float32),
            pltpu.VMEM((n_vcol, groups, gw, wide), jnp.int16),
            pltpu.VMEM((n_vcol, groups, 1, wide), jnp.float32),
            pltpu.VMEM((2, groups, gw, wide), jnp.int16),
            pltpu.VMEM((2, groups, 1, wide), jnp.float32),
            pltpu.VMEM((groups, gw, wide), jnp.int16),
            pltpu.VMEM((groups, 1, wide), jnp.float32),
            pltpu.VMEM((groups, gw, wide), jnp.int16),
            pltpu.VMEM((groups, 1, wide), jnp.float32),
            pltpu.VMEM((ch, n_vrow, vs, n), jnp.int16),
            pltpu.VMEM((ch, n_vrow, 1, n), jnp.float32),
            pltpu.VMEM((n_vrow, ch, vs, n), jnp.int16),
            pltpu.VMEM((n_vrow, ch, 1, n), jnp.float32),
            pltpu.VMEM((n_vcol, 1, 128), jnp.int32),
            pltpu.VMEM((1, 1, 128), jnp.int32),
            pltpu.SMEM((n_vcol, 1, 128), jnp.int32),
            pltpu.SMEM((n_vrow, 1, 128), jnp.int32),
            dma((occ,)),
            dma((2,)),
            dma((2,)),
            dma((3, groups)),
            dma((3, groups)),
            dma((3, groups)),
            dma((3, groups)),
            dma((4,)),
            dma((4,)),
            dma((n_vcol, groups)),
            dma((2, groups)),
            dma((n_vcol, groups)),
            dma((2, groups)),
            dma((groups,)),
            dma((groups,)),
            dma((groups,)),
            dma((groups,)),
            dma((ch, n_vrow)),
            dma((n_vrow, ch)),
            dma((ch, n_vrow)),
            dma((n_vrow, ch)),
            pltpu.SemaphoreType.REGULAR((2,)),
        ],
        compiler_params=pltpu.CompilerParams(collective_id=0, has_side_effects=True, vmem_limit_bytes=24 * 2**20),
    )(blocks, block_ids, block_counts)
    return (out * (1.0 / (n_field * SBLK * BLOCK))).reshape(vs, ch, n_vrow, 1, ch, vs)


def solution(mesh):
    placed = (
        P(("vrow", "vcol"), "field", None, None),
        P(("vrow", "vcol"), "field", None),
        P(("vrow", "vcol"), "field"),
    )
    square = mesh.shape["field"] == 4 and mesh.shape["vcol"] == 4 and mesh.shape["vrow"] == 2
    return jax.shard_map(
        on_square_device if square else on_any_device,
        mesh=mesh,
        in_specs=placed,
        out_specs=P(("vrow", "field"), None, None, "vcol", None, None),
        check_vma=False,
    )
```

```python
import functools

import jax
import jax.numpy as jnp
from jax import lax
from jax.experimental import pallas as pl
from jax.experimental.pallas import tpu as pltpu
from jax.sharding import PartitionSpec as P

SBLK = 12
BLOCK = 256
MAX_PIECES = 4
STEPS_AHEAD = 2
AHEAD = 4
PLAN = (
    "S0", "o0", "S1", "X0", "Y0", "S2", "o1", "X1", "Y1", "s0",
    "s1", "o2", "X2", "Y2", "x0", "y0", "o3", "X3", "Y3", "S3",
    "x1", "y1", "s2", "f0", "t0", "D0", "x2", "y2", "f1", "D1",
    "x3", "t1", "f2", "D2", "y3", "t2", "d0", "f3", "D3", "d1",
    "t3", "d2", "d3", "s3",
)
LEVELS = 65535.0
HALF = 32768
MESH = pl.DeviceIdType.MESH


def partner(q, d, n):
    if n == 4:
        return (q + 1 - 2 * lax.rem(q, 2), lax.rem(q + 2, 4), 3 - q)[d - 1]
    return lax.rem(q + d, n)


def any_kernel(
    dims, scale, data, ids, counts, out, meta, rows, raw_cols, cols, part, code, tops, got, got_tops, mine_sum, rmeta, cmeta, rids, cids,
    row_local, meta_local,
    row_send, row_recv, col_send, col_recv, rm_send, rm_recv, cm_send, cm_recv,
    part_send, part_recv, top_send, top_recv,
):
    n_field, n_vrow, n_vcol, pieces, occ, width, per_chunk = dims
    f, r, q = lax.axis_index("field"), lax.axis_index("vrow"), lax.axis_index("vcol")
    relay = n_vcol == 4

    barrier = pltpu.get_barrier_semaphore()
    for d in range(1, n_vcol):
        pl.semaphore_signal(barrier, inc=1, device_id={"vcol": partner(q, d, n_vcol)}, device_id_type=MESH)
    for d in range(1, n_vrow):
        pl.semaphore_signal(barrier, inc=1, device_id={"vrow": lax.rem(r + d, n_vrow)}, device_id_type=MESH)
    for d in range(1, n_field):
        pl.semaphore_signal(barrier, inc=1, device_id={"field": lax.rem(f + d, n_field)}, device_id_type=MESH)

    meta[...] = jnp.full_like(meta, -1)
    slots = lax.broadcasted_iota(jnp.int32, (1, occ), 1)
    meta[:, 0:occ] = jnp.where(slots < counts[...], ids[0], -1)
    own = pltpu.make_async_copy(data, rows.at[0], row_local.at[0])
    own.start()
    for v in range(n_vrow):
        cols[v, occ] = jnp.zeros_like(cols[v, occ])

    pl.semaphore_wait(barrier, n_vcol + n_vrow + n_field - 3)

    own_r = pltpu.make_async_copy(meta, rids.at[0], meta_local.at[0])
    own_r.start()
    own_c = pltpu.make_async_copy(meta, cids.at[0], meta_local.at[1])
    own_c.start()

    def span(p):
        return pl.ds(p * width, width)

    sends = []

    def send(src, dst, s, w, where):
        c = pltpu.make_async_remote_copy(
            src_ref=src, dst_ref=dst, send_sem=s, recv_sem=w, device_id=where, device_id_type=MESH
        )
        c.start()
        sends.append(c)
        return c

    row_meta, col_meta, row_copy, col_copy = {}, {}, {}, {}

    def send_rows(p):
        for d in range(1, 3 if relay else n_vcol):
            to = {"vcol": partner(q, d, n_vcol)}
            row_copy[d, p] = send(data.at[span(p)], rows.at[d, span(p)], row_send.at[d, p], row_recv.at[d, p], to)

    for d in range(1, n_vrow):
        to = {"vrow": lax.rem(r + d, n_vrow)}
        col_meta[d] = send(meta, cmeta.at[d], cm_send.at[d], cm_recv.at[d], to)
    for d in range(1, n_vcol):
        to = {"vcol": partner(q, d, n_vcol)}
        row_meta[d] = send(meta, rmeta.at[d], rm_send.at[d], rm_recv.at[d], to)
    for p in range(pieces):
        for d in range(1, n_vrow):
            to = {"vrow": lax.rem(r + d, n_vrow)}
            col_copy[d, p] = send(
                data.at[span(p)],
                raw_cols.at[d, span(p)],
                col_send.at[d, p], col_recv.at[d, p], to,
            )
        if p < (STEPS_AHEAD if relay else pieces):
            send_rows(p)

    own.wait()
    own_r.wait()
    own_c.wait()
    for d in range(1, n_vrow):
        col_meta[d].wait_recv()
        c = pltpu.make_async_copy(cmeta.at[d], cids.at[d], meta_local.at[1])
        c.start()
        c.wait()
    for d in range(1, n_vrow):
        for p in range(pieces):
            col_copy[d, p].wait_recv()
    ch, vs = rows.shape[3], rows.shape[1]
    n = ch * vs
    to_row = lax.broadcasted_iota(jnp.int32, (n, n), 0)
    from_row = lax.broadcasted_iota(jnp.int32, (n, n), 1)
    order = jnp.where(from_row == lax.rem(to_row, vs) * ch + to_row // vs, 1.0, 0.0).astype(jnp.bfloat16)
    for v in range(n_vrow):
        for o in range(occ):
            block = (raw_cols[v, :, o] if v else rows[0, :, o]).reshape(n, rows.shape[-1])
            turned = jnp.dot(order, block, preferred_element_type=jnp.float32)
            cols[v, o] = turned.astype(jnp.bfloat16)

    match = {}
    part_sends = []

    def matches(d):
        if d:
            row_meta[d].wait_recv()
            c = pltpu.make_async_copy(rmeta.at[d], rids.at[d], meta_local.at[0])
            c.start()
            c.wait()
        theirs = [[cids[v, 0, o] for o in range(occ)] for v in range(n_vrow)]
        found = []
        for o in range(occ):
            mine = rids[d, 0, o]
            for v in range(n_vrow):
                m = jnp.int32(occ)
                for k in range(occ):
                    m = jnp.where((mine >= 0) & (mine == theirs[v][k]), jnp.int32(k), m)
                found.append(m)
        return found

    def compute(d, p):
        if d not in match:
            match[d] = matches(d)
        for v in range(n_vrow):
            acc = None
            for o in range(occ):
                lhs = rows[d, p * width : (p + 1) * width, o].reshape(ch * width, rows.shape[-1])
                rhs = cols[v, match[d][o * n_vrow + v]]
                t = lax.dot_general(lhs, rhs, (((1,), (1,)), ((), ())), preferred_element_type=jnp.float32)
                acc = t if acc is None else acc + t
            n = acc.shape[1]
            at = pl.multiple_of(lax.rem(r + v, n_vrow) * n, n)
            part[d, p, :, pl.ds(at, n)] = acc
            top = jnp.max(acc, axis=0, keepdims=True)
            inverse = jnp.where(top > 0, 1.0 / top, 0.0)
            level = ((acc * inverse) * LEVELS + 0.5).astype(jnp.int32) - HALF
            code[d, p, :, pl.ds(at, n)] = level.astype(jnp.int16)
            tops[d, p, :, pl.ds(at, n)] = top
        s = q if d == 0 else partner(q, d, n_vcol)
        g = s * pieces + p
        dest = g // per_chunk
        place = g - dest * per_chunk
        to = {"field": dest}
        c = pltpu.make_async_remote_copy(
            src_ref=code.at[d, p], dst_ref=got.at[f, place],
            send_sem=part_send.at[d, p], recv_sem=part_recv.at[f, place],
            device_id=to, device_id_type=MESH,
        )
        t = pltpu.make_async_remote_copy(
            src_ref=tops.at[d, p], dst_ref=got_tops.at[f, place],
            send_sem=top_send.at[d, p], recv_sem=top_recv.at[f, place],
            device_id=to, device_id_type=MESH,
        )

        @pl.when(dest != f)
        def _():
            t.start()
            c.start()

        @pl.when(dest == f)
        def _():
            mine_sum[place] = part[d, p]

        part_sends.append((dest, c, t))

    def forward(p):
        first = pl.ds(p * width, width // 2)
        second = pl.ds(p * width + width // 2, width - width // 2)
        row_copy[1, p].wait_recv()
        a = send(rows.at[1, first], rows.at[3, first],
                 row_send.at[3, p], row_recv.at[3, p], {"vcol": partner(q, 2, 4)})
        row_copy[2, p].wait_recv()
        b = send(rows.at[2, second], rows.at[3, second],
                 row_send.at[0, p], row_recv.at[0, p], {"vcol": partner(q, 1, 4)})
        row_copy[3, p] = (a, b)
        if p + STEPS_AHEAD < pieces:
            send_rows(p + STEPS_AHEAD)

    compute(0, 0)
    for p in range(pieces):
        if relay:
            forward(p)
        for d in range(1, 3 if relay else n_vcol):
            if not relay:
                row_copy[d, p].wait_recv()
            compute(d, p)
        if p + 1 < pieces:
            compute(0, p + 1)
        if relay and p:
            for c in row_copy[3, p - 1]:
                c.wait_recv()
            compute(3, p - 1)
    if relay:
        for c in row_copy[3, pieces - 1]:
            c.wait_recv()
        compute(3, pieces - 1)

    for place in range(per_chunk):
        total = mine_sum[place]
        for d in range(1, n_field):
            src = lax.rem(f + d, n_field)
            for buf, land, gone, came in (
                (code, got, part_send, part_recv), (tops, got_tops, top_send, top_recv),
            ):
                pltpu.make_async_remote_copy(
                    src_ref=buf.at[0, 0], dst_ref=land.at[src, place],
                    send_sem=gone.at[0, 0], recv_sem=came.at[src, place],
                    device_id={"field": src}, device_id_type=MESH,
                ).wait_recv()
            level = (got[src, place].astype(jnp.int32) + HALF).astype(jnp.float32)
            total = total + level * (got_tops[src, place] * (1.0 / LEVELS))
        parts = n_vrow * ch
        for k in range(parts):
            out[pl.ds(place * ch * width * parts + k, ch * width, parts), :] = total[:, k * vs : (k + 1) * vs]
    for c in sends:
        c.wait_send()
    for dest, c, t in part_sends:
        @pl.when(dest != f)
        def _():
            c.wait_send()
            t.wait_send()


def on_any_device(blocks, block_ids, block_counts):
    n_field, n_vrow, n_vcol = (lax.axis_size(a) for a in ("field", "vrow", "vcol"))
    vs, occ, ch, x = blocks.shape
    chunk = n_vcol * vs // n_field
    width = min(vs // MAX_PIECES, chunk)
    pieces = vs // width
    per_chunk = chunk // width
    data = blocks
    c = ch * vs
    wide = n_vrow * c
    dims = (n_field, n_vrow, n_vcol, pieces, occ, width, per_chunk)
    dma = pltpu.SemaphoreType.DMA
    scale = 1.0 / (n_field * SBLK * BLOCK)
    out = pl.pallas_call(
        functools.partial(any_kernel, dims, scale),
        out_shape=jax.ShapeDtypeStruct((chunk * ch * n_vrow * ch, vs), jnp.float32),
        in_specs=[pl.BlockSpec(memory_space=pl.ANY)] + [pl.BlockSpec(memory_space=pltpu.VMEM)] * 2,
        out_specs=pl.BlockSpec(memory_space=pltpu.VMEM),
        scratch_shapes=[
            pltpu.VMEM((1, 128), jnp.int32),
            pltpu.VMEM((n_vcol, vs, occ, ch, x), jnp.bfloat16),
            pltpu.VMEM((n_vrow, vs, occ, ch, x), jnp.bfloat16),
            pltpu.VMEM((n_vrow, occ + 1, ch * vs, x), jnp.bfloat16),
            pltpu.VMEM((n_vcol, pieces, ch * width, wide), jnp.float32),
            pltpu.VMEM((n_vcol, pieces, ch * width, wide), jnp.int16),
            pltpu.VMEM((n_vcol, pieces, 1, wide), jnp.float32),
            pltpu.VMEM((n_field, per_chunk, ch * width, wide), jnp.int16),
            pltpu.VMEM((n_field, per_chunk, 1, wide), jnp.float32),
            pltpu.VMEM((per_chunk, ch * width, wide), jnp.float32),
            pltpu.VMEM((n_vcol, 1, 128), jnp.int32),
            pltpu.VMEM((n_vrow, 1, 128), jnp.int32),
            pltpu.SMEM((n_vcol, 1, 128), jnp.int32),
            pltpu.SMEM((n_vrow, 1, 128), jnp.int32),
            dma((1,)),
            dma((2,)),
            dma((n_vcol, pieces)),
            dma((n_vcol, pieces)),
            dma((n_vrow, pieces)),
            dma((n_vrow, pieces)),
            dma((n_vcol,)),
            dma((n_vcol,)),
            dma((n_vrow,)),
            dma((n_vrow,)),
            dma((n_vcol, pieces)),
            dma((n_field, per_chunk)),
            dma((n_vcol, pieces)),
            dma((n_field, per_chunk)),
        ],
        compiler_params=pltpu.CompilerParams(collective_id=1, has_side_effects=True),
    )(data, block_ids, block_counts)
    return (out * scale).reshape(chunk, ch, n_vrow, 1, ch, vs)


def square_kernel(
    dims, data, ids, counts, out,
    meta, raw, cols, rows, mine, hold, code, tops, got, got_tops, code2, tops2, got2, got2_tops, turn, turn_tops, turned, turned_tops,
    rmeta, cmeta, rids, cids,
    raw_sem, meta_local, col_sem, own_send, own_recv, far_send, far_recv,
    m_send, m_recv, part_send, part_recv, top_send, top_recv, part2_send, part2_recv, top2_send, top2_recv,
    turn_send, turn_recv, ttop_send, ttop_recv, two,
):
    n_field, n_vrow, n_vcol, groups, occ, vs, ch = dims
    n, half = cols.shape[3], cols.shape[4]
    gw = n // groups
    f, r, q = lax.axis_index("field"), lax.axis_index("vrow"), lax.axis_index("vcol")
    beside = f + 1 - 2 * lax.rem(f, 2)
    inner = (f > 0) & (f + 1 < n_field)
    over = [q, partner(q, 1, 4), partner(q, 2, 4), partner(q, 3, 4)]
    twin = {"vrow": 1 - r}
    near = {1: {"vcol": over[1]}, 2: {"vcol": over[2]}}
    odd = lax.rem(q // 2 + q, 2)
    place = [1 - odd, odd]

    barrier = pltpu.get_barrier_semaphore()
    for to in (twin, near[1], near[2]):
        pl.semaphore_signal(barrier, inc=1, device_id=to, device_id_type=MESH)

    @pl.when(f + 1 < n_field)
    def _():
        pl.semaphore_signal(barrier, inc=1, device_id={"field": lax.rem(f + 1, n_field)}, device_id_type=MESH)

    @pl.when(f > 0)
    def _():
        pl.semaphore_signal(barrier, inc=1, device_id={"field": lax.rem(f + n_field - 1, n_field)}, device_id_type=MESH)

    loads = []
    for o in range(occ):
        c = pltpu.make_async_copy(data.at[:, o], raw.at[o], raw_sem.at[o])
        c.start()
        loads.append(c)
    meta[...] = jnp.full_like(meta, -1)
    slots = lax.broadcasted_iota(jnp.int32, (1, occ), 1)
    meta[:, 0:occ] = jnp.where(slots < counts[...], ids[0], -1)
    own_r = pltpu.make_async_copy(meta, rids.at[0], meta_local.at[0])
    own_r.start()
    own_c = pltpu.make_async_copy(meta, cids.at[0], meta_local.at[1])
    own_c.start()
    for b in range(2):
        for v in range(n_vrow):
            cols[b, v, occ] = jnp.zeros_like(cols[b, v, occ])
    to_row = lax.broadcasted_iota(jnp.int32, (n, n), 0)
    from_row = lax.broadcasted_iota(jnp.int32, (n, n), 1)
    order = jnp.where(from_row == lax.rem(to_row, vs) * ch + to_row // vs, 1.0, 0.0).astype(jnp.bfloat16)
    for o in range(occ):
        loads[o].wait()
        sorted_rows = jnp.dot(order, raw[o].reshape(n, 2 * half), preferred_element_type=jnp.float32)
        for b in range(2):
            cols[place[b], 0, o] = sorted_rows[:, b * half : (b + 1) * half].astype(jnp.bfloat16)
    own_r.wait()
    own_c.wait()

    @pl.when((f > 0) & (f + 1 < n_field))
    def _():
        pl.semaphore_wait(barrier, 5)

    @pl.when((f == 0) | (f + 1 == n_field))
    def _():
        pl.semaphore_wait(barrier, 4)

    sends = []

    def send(src, dst, s, t, where):
        c = pltpu.make_async_remote_copy(
            src_ref=src, dst_ref=dst, send_sem=s, recv_sem=t, device_id=where, device_id_type=MESH
        )
        c.start()
        sends.append(c)
        return c

    @pl.when(inner)
    def _():
        pl.semaphore_signal(two, inc=1, device_id={"field": n_field - 1 - f}, device_id_type=MESH)

    live = pl.ds(0, occ)
    twin_copy = send(cols.at[:, 0, live], cols.at[:, 1, live], col_sem.at[0], col_sem.at[1], twin)
    c_meta = send(meta, cmeta.at[0], m_send.at[0], m_recv.at[0], twin)
    r_meta = {}
    for d in (1, 2):
        r_meta[d] = send(meta, rmeta.at[d], m_send.at[d], m_recv.at[d], near[d])
    own_copy, far_copy = {}, {}

    def span(g):
        return pl.ds(g * gw, gw)

    def send_own(g):
        for d in (1, 2):
            own_copy[d, g] = send(
                cols.at[2 - d, 0, live, span(g)], rows.at[d - 1, :, span(g)], own_send.at[d, g], own_recv.at[d, g], near[d]
            )

    def send_far(g):
        for d in (1, 2):
            far_copy[3 - d, g] = send(
                rows.at[d - 1, :, span(g)], rows.at[4 - d, :, span(g)], far_send.at[3 - d, g], far_recv.at[3 - d, g],
                near[3 - d],
            )

    for g in range(min(AHEAD, groups)):
        send_own(g)

    @pl.when(inner)
    def _():
        pl.semaphore_wait(two, 1)

    c_meta.wait_recv()
    c = pltpu.make_async_copy(cmeta.at[0], cids.at[1], meta_local.at[1])
    c.start()
    c.wait()
    theirs = [[cids[v, 0, o] for o in range(occ)] for v in range(n_vrow)]

    def matches(d):
        if d:
            if d > 1:
                r_meta[d].wait_recv()
            c = pltpu.make_async_copy(rmeta.at[d], rids.at[d], meta_local.at[0])
            c.start()
            c.wait()
        found = {}
        for o in range(occ):
            own = rids[d, 0, o]
            for v in range(n_vrow):
                m = jnp.int32(occ)
                for k in range(occ):
                    m = jnp.where((own >= 0) & (own == theirs[v][k]), jnp.int32(k), m)
                found[o, v] = m
        return found

    match = {}
    part_sends = []

    def encode(acc):
        top = jnp.max(acc, axis=0, keepdims=True)
        inverse = jnp.where(top > 0, 1.0 / top, 0.0)
        level = ((acc * inverse) * LEVELS + 0.5).astype(jnp.int32) - HALF
        return level.astype(jnp.int16), top

    def decode(level, top):
        return (level.astype(jnp.int32) + HALF).astype(jnp.float32) * (top * (1.0 / LEVELS))

    def first_hop(dest, d, g):
        i = jnp.where(dest == beside, 0, 1 + lax.rem(dest, 2))
        to = {"field": beside}
        return (
            pltpu.make_async_remote_copy(
                src_ref=code.at[d, g], dst_ref=got.at[i, g],
                send_sem=part_send.at[d, g], recv_sem=part_recv.at[i, g], device_id=to, device_id_type=MESH,
            ),
            pltpu.make_async_remote_copy(
                src_ref=tops.at[d, g], dst_ref=got_tops.at[i, g],
                send_sem=top_send.at[d, g], recv_sem=top_recv.at[i, g], device_id=to, device_id_type=MESH,
            ),
        )

    def came(i, g):
        for c in (
            pltpu.make_async_remote_copy(
                src_ref=code.at[0, g], dst_ref=got.at[i, g], send_sem=part_send.at[0, g], recv_sem=part_recv.at[i, g],
                device_id={"field": beside}, device_id_type=MESH,
            ),
            pltpu.make_async_remote_copy(
                src_ref=tops.at[0, g], dst_ref=got_tops.at[i, g], send_sem=top_send.at[0, g], recv_sem=top_recv.at[i, g],
                device_id={"field": beside}, device_id_type=MESH,
            ),
        ):
            c.wait_recv()
        return decode(got[i, g], got_tops[i, g])

    def second_hop(i, g):
        to = {"field": lax.rem(n_field - 2 * (f // 2) - 2, n_field) + i}
        return (
            pltpu.make_async_remote_copy(
                src_ref=code2.at[i, g], dst_ref=got2.at[g], send_sem=part2_send.at[i, g], recv_sem=part2_recv.at[g],
                device_id=to, device_id_type=MESH,
            ),
            pltpu.make_async_remote_copy(
                src_ref=tops2.at[i, g], dst_ref=got2_tops.at[g], send_sem=top2_send.at[i, g], recv_sem=top2_recv.at[g],
                device_id=to, device_id_type=MESH,
            ),
        )

    def merge(d, g):
        @pl.when(over[d] == f)
        def _():
            mine[g] += came(0, g)

        @pl.when(inner & (over[d] // 2 != f // 2))
        def _():
            i = lax.rem(over[d], 2)
            code2[i, g], tops2[i, g] = encode(hold[i, g] + came(1 + i, g))
            for c in reversed(second_hop(i, g)):
                c.start()

    def summed(g):
        for c in second_hop(0, g):
            c.wait_recv()
        return mine[g] + decode(got2[g], got2_tops[g])

    def compute(d, g):
        if d not in match:
            match[d] = matches(d)
        at = pl.ds(g * gw, gw)
        halves = []
        for v in range(n_vrow):
            acc = None
            for o in range(occ):
                k = match[d][o, v]
                if d in (1, 2):
                    lhs, rhs = rows[d - 1, o, at], cols[d - 1, v, k]
                else:
                    lhs = [cols[b, 0, o, at] if d == 0 else rows[2 + b, o, at] for b in range(2)]
                    lhs = jnp.concatenate(lhs, axis=1)
                    rhs = jnp.concatenate([cols[b, v, k] for b in range(2)], axis=1)
                t = lax.dot_general(lhs, rhs, (((1,), (1,)), ((), ())), preferred_element_type=jnp.float32)
                acc = t if acc is None else acc + t
            halves.append(acc)
        dest = over[d]

        kept = inner & (dest // 2 != f // 2)
        leaves = (dest != f) & jnp.logical_not(kept)
        c, t = first_hop(dest, d, g)

        def at(v):
            return pl.ds(pl.multiple_of(lax.rem(r + v, n_vrow) * n, n), n)

        @pl.when(dest == f)
        def _():
            for v in range(n_vrow):
                mine[g, :, at(v)] = halves[v]

        @pl.when(kept)
        def _():
            for v in range(n_vrow):
                hold[lax.rem(dest, 2), g, :, at(v)] = halves[v]

        @pl.when(leaves)
        def _():
            for v in range(n_vrow):
                code[d, g, :, at(v)], tops[d, g, :, at(v)] = encode(halves[v])
            t.start()
            c.start()

        part_sends.append((leaves, c, t))

    swaps = (f == over[1]) | (f == over[2])
    turn_copies = {}

    def swap(a):
        for b in range(n_vrow):
            to = {"field": q, "vrow": b, "vcol": f}
            turn_copies[a, b] = (
                pltpu.make_async_remote_copy(
                    src_ref=turn.at[a, b], dst_ref=turned.at[r, a],
                    send_sem=turn_send.at[a, b], recv_sem=turn_recv.at[r, a],
                    device_id=to, device_id_type=MESH,
                ),
                pltpu.make_async_remote_copy(
                    src_ref=turn_tops.at[a, b], dst_ref=turned_tops.at[r, a],
                    send_sem=ttop_send.at[a, b], recv_sem=ttop_recv.at[r, a],
                    device_id=to, device_id_type=MESH,
                ),
            )

        @pl.when(swaps)
        def _():
            total = summed(a)
            mine[a] = total
            for b in range(n_vrow):
                turn[a, b], turn_tops[a, b] = encode(total[:, b * n : (b + 1) * n])
                for c in reversed(turn_copies[a, b]):
                    c.start()

    def step(kind, i):
        if kind in "SXYD":
            compute("SXYD".index(kind), i)
        elif kind in "sxyd":
            merge("sxyd".index(kind), i)
        elif kind == "o":
            for d in (1, 2):
                own_copy[d, i].wait_recv()
            if i == 0:
                r_meta[1].wait_recv()
                r_meta[3] = send(rmeta.at[1], rmeta.at[3], m_send.at[3], m_recv.at[3], near[2])
            send_far(i)
            if i + AHEAD < groups:
                send_own(i + AHEAD)
        elif kind == "f":
            for d in (1, 2):
                far_copy[d, i].wait_recv()
        else:
            swap(i)

    twin_copy.wait_recv()
    for name in PLAN:
        step(name[0], int(name[1:]))

    parts = n_vrow * ch

    def put(a, k, values):
        out[pl.ds(a * parts + k, vs, ch * parts), :] = values

    def held(a, k):
        each = [mine[g, :, k * vs : (k + 1) * vs] for g in range(a * groups // ch, (a + 1) * groups // ch)]
        return jnp.concatenate(each, axis=0)

    @pl.when(jnp.logical_not(swaps))
    def _():
        for a in range(ch):
            for g in range(a * groups // ch, (a + 1) * groups // ch):
                total = summed(g)
                at = (g * gw) % vs
                for k in range(parts):
                    out[pl.ds((at * ch + a) * parts + k, gw, ch * parts), :] = total[:, k * vs : (k + 1) * vs]

    @pl.when(swaps)
    def _():
        for b in range(ch):
            for v in range(n_vrow):
                each = []
                for g in range(b * groups // ch, (b + 1) * groups // ch):
                    for land, came, gone, buf in (
                        (turned, turn_recv, turn_send, turn), (turned_tops, ttop_recv, ttop_send, turn_tops),
                    ):
                        pltpu.make_async_remote_copy(
                            src_ref=buf.at[0, 0], dst_ref=land.at[v, g],
                            send_sem=gone.at[0, 0], recv_sem=came.at[v, g],
                            device_id={"field": q, "vrow": r, "vcol": f}, device_id_type=MESH,
                        ).wait_recv()
                    each.append(decode(turned[v, g], turned_tops[v, g]))
                back = jnp.transpose(jnp.concatenate(each, axis=0))
                k = v * ch + b
                for a in range(ch):
                    put(a, k, held(a, k) + back[a * vs : (a + 1) * vs])
        for c, t in turn_copies.values():
            c.wait_send()
            t.wait_send()

    for c in sends:
        c.wait_send()
    for sent, c, t in part_sends:
        @pl.when(sent)
        def _():
            c.wait_send()
            t.wait_send()

    @pl.when(inner)
    def _():
        for i in range(2):
            for g in range(groups):
                for c in second_hop(i, g):
                    c.wait_send()


def on_square_device(blocks, block_ids, block_counts):
    n_field, n_vrow, n_vcol = (lax.axis_size(a) for a in ("field", "vrow", "vcol"))
    vs, occ, ch, x = blocks.shape
    n = ch * vs
    groups = 4
    gw = n // groups
    half = x // 2
    dims = (n_field, n_vrow, n_vcol, groups, occ, vs, ch)
    dma = pltpu.SemaphoreType.DMA
    wide = n_vrow * n
    out = pl.pallas_call(
        functools.partial(square_kernel, dims),
        out_shape=jax.ShapeDtypeStruct((vs * ch * n_vrow * ch, vs), jnp.float32),
        in_specs=[pl.BlockSpec(memory_space=pl.ANY)] + [pl.BlockSpec(memory_space=pltpu.VMEM)] * 2,
        out_specs=pl.BlockSpec(memory_space=pltpu.VMEM),
        scratch_shapes=[
            pltpu.VMEM((1, 128), jnp.int32),
            pltpu.VMEM((occ, vs, ch, x), jnp.bfloat16),
            pltpu.VMEM((2, n_vrow, occ + 1, n, half), jnp.bfloat16),
            pltpu.VMEM((4, occ, n, half), jnp.bfloat16),
            pltpu.VMEM((groups, gw, wide), jnp.float32),
            pltpu.VMEM((2, groups, gw, wide), jnp.float32),
            pltpu.VMEM((n_vcol, groups, gw, wide), jnp.int16),
            pltpu.VMEM((n_vcol, groups, 1, wide), jnp.float32),
            pltpu.VMEM((3, groups, gw, wide), jnp.int16),
            pltpu.VMEM((3, groups, 1, wide), jnp.float32),
            pltpu.VMEM((2, groups, gw, wide), jnp.int16),
            pltpu.VMEM((2, groups, 1, wide), jnp.float32),
            pltpu.VMEM((groups, gw, wide), jnp.int16),
            pltpu.VMEM((groups, 1, wide), jnp.float32),
            pltpu.VMEM((groups, n_vrow, gw, n), jnp.int16),
            pltpu.VMEM((groups, n_vrow, 1, n), jnp.float32),
            pltpu.VMEM((n_vrow, groups, gw, n), jnp.int16),
            pltpu.VMEM((n_vrow, groups, 1, n), jnp.float32),
            pltpu.VMEM((n_vcol, 1, 128), jnp.int32),
            pltpu.VMEM((1, 1, 128), jnp.int32),
            pltpu.SMEM((n_vcol, 1, 128), jnp.int32),
            pltpu.SMEM((n_vrow, 1, 128), jnp.int32),
            dma((occ,)),
            dma((2,)),
            dma((2,)),
            dma((3, groups)),
            dma((3, groups)),
            dma((3, groups)),
            dma((3, groups)),
            dma((4,)),
            dma((4,)),
            dma((n_vcol, groups)),
            dma((3, groups)),
            dma((n_vcol, groups)),
            dma((3, groups)),
            dma((2, groups)),
            dma((groups,)),
            dma((2, groups)),
            dma((groups,)),
            dma((groups, n_vrow)),
            dma((n_vrow, groups)),
            dma((groups, n_vrow)),
            dma((n_vrow, groups)),
            pltpu.SemaphoreType.REGULAR,
        ],
        compiler_params=pltpu.CompilerParams(collective_id=0, has_side_effects=True, vmem_limit_bytes=24 * 2**20),
    )(blocks, block_ids, block_counts)
    return (out * (1.0 / (n_field * SBLK * BLOCK))).reshape(vs, ch, n_vrow, 1, ch, vs)


def solution(mesh):
    placed = (
        P(("vrow", "vcol"), "field", None, None),
        P(("vrow", "vcol"), "field", None),
        P(("vrow", "vcol"), "field"),
    )
    square = mesh.shape["field"] == 4 and mesh.shape["vcol"] == 4 and mesh.shape["vrow"] == 2
    return jax.shard_map(
        on_square_device if square else on_any_device,
        mesh=mesh,
        in_specs=placed,
        out_specs=P(("vrow", "field"), None, None, "vcol", None, None),
        check_vma=False,
    )
```

```python
import functools

import jax
import jax.numpy as jnp
from jax import lax
from jax.experimental import pallas as pl
from jax.experimental.pallas import tpu as pltpu
from jax.sharding import PartitionSpec as P

SBLK = 12
BLOCK = 256
MAX_PIECES = 4
STEPS_AHEAD = 2
AHEAD = 4
PLAN = (
    "S0", "o0", "S1", "X0", "Y0", "S2", "o1", "X1", "Y1", "s0",
    "s1", "o2", "X2", "Y2", "x0", "y0", "o3", "X3", "Y3", "S3",
    "x1", "y1", "s2", "f0", "t0", "D0", "x2", "y2", "f1", "D1",
    "x3", "t1", "f2", "D2", "y3", "t2", "d0", "f3", "D3", "d1",
    "t3", "d2", "d3", "s3",
)
LEVELS = 65535.0
HALF = 32768
MESH = pl.DeviceIdType.MESH


def partner(q, d, n):
    if n == 4:
        return (q + 1 - 2 * lax.rem(q, 2), lax.rem(q + 2, 4), 3 - q)[d - 1]
    return lax.rem(q + d, n)


def any_kernel(
    dims, scale, data, ids, counts, out, meta, rows, raw_cols, cols, part, code, tops, got, got_tops, mine_sum, rmeta, cmeta, rids, cids,
    row_local, meta_local,
    row_send, row_recv, col_send, col_recv, rm_send, rm_recv, cm_send, cm_recv,
    part_send, part_recv, top_send, top_recv,
):
    n_field, n_vrow, n_vcol, pieces, occ, width, per_chunk = dims
    f, r, q = lax.axis_index("field"), lax.axis_index("vrow"), lax.axis_index("vcol")
    relay = n_vcol == 4

    barrier = pltpu.get_barrier_semaphore()
    for d in range(1, n_vcol):
        pl.semaphore_signal(barrier, inc=1, device_id={"vcol": partner(q, d, n_vcol)}, device_id_type=MESH)
    for d in range(1, n_vrow):
        pl.semaphore_signal(barrier, inc=1, device_id={"vrow": lax.rem(r + d, n_vrow)}, device_id_type=MESH)
    for d in range(1, n_field):
        pl.semaphore_signal(barrier, inc=1, device_id={"field": lax.rem(f + d, n_field)}, device_id_type=MESH)

    meta[...] = jnp.full_like(meta, -1)
    slots = lax.broadcasted_iota(jnp.int32, (1, occ), 1)
    meta[:, 0:occ] = jnp.where(slots < counts[...], ids[0], -1)
    own = pltpu.make_async_copy(data, rows.at[0], row_local.at[0])
    own.start()
    for v in range(n_vrow):
        cols[v, occ] = jnp.zeros_like(cols[v, occ])

    pl.semaphore_wait(barrier, n_vcol + n_vrow + n_field - 3)

    own_r = pltpu.make_async_copy(meta, rids.at[0], meta_local.at[0])
    own_r.start()
    own_c = pltpu.make_async_copy(meta, cids.at[0], meta_local.at[1])
    own_c.start()

    def span(p):
        return pl.ds(p * width, width)

    sends = []

    def send(src, dst, s, w, where):
        c = pltpu.make_async_remote_copy(
            src_ref=src, dst_ref=dst, send_sem=s, recv_sem=w, device_id=where, device_id_type=MESH
        )
        c.start()
        sends.append(c)
        return c

    row_meta, col_meta, row_copy, col_copy = {}, {}, {}, {}

    def send_rows(p):
        for d in range(1, 3 if relay else n_vcol):
            to = {"vcol": partner(q, d, n_vcol)}
            row_copy[d, p] = send(data.at[span(p)], rows.at[d, span(p)], row_send.at[d, p], row_recv.at[d, p], to)

    for d in range(1, n_vrow):
        to = {"vrow": lax.rem(r + d, n_vrow)}
        col_meta[d] = send(meta, cmeta.at[d], cm_send.at[d], cm_recv.at[d], to)
    for d in range(1, n_vcol):
        to = {"vcol": partner(q, d, n_vcol)}
        row_meta[d] = send(meta, rmeta.at[d], rm_send.at[d], rm_recv.at[d], to)
    for p in range(pieces):
        for d in range(1, n_vrow):
            to = {"vrow": lax.rem(r + d, n_vrow)}
            col_copy[d, p] = send(
                data.at[span(p)],
                raw_cols.at[d, span(p)],
                col_send.at[d, p], col_recv.at[d, p], to,
            )
        if p < (STEPS_AHEAD if relay else pieces):
            send_rows(p)

    own.wait()
    own_r.wait()
    own_c.wait()
    for d in range(1, n_vrow):
        col_meta[d].wait_recv()
        c = pltpu.make_async_copy(cmeta.at[d], cids.at[d], meta_local.at[1])
        c.start()
        c.wait()
    for d in range(1, n_vrow):
        for p in range(pieces):
            col_copy[d, p].wait_recv()
    ch, vs = rows.shape[3], rows.shape[1]
    n = ch * vs
    to_row = lax.broadcasted_iota(jnp.int32, (n, n), 0)
    from_row = lax.broadcasted_iota(jnp.int32, (n, n), 1)
    order = jnp.where(from_row == lax.rem(to_row, vs) * ch + to_row // vs, 1.0, 0.0).astype(jnp.bfloat16)
    for v in range(n_vrow):
        for o in range(occ):
            block = (raw_cols[v, :, o] if v else rows[0, :, o]).reshape(n, rows.shape[-1])
            turned = jnp.dot(order, block, preferred_element_type=jnp.float32)
            cols[v, o] = turned.astype(jnp.bfloat16)

    match = {}
    part_sends = []

    def matches(d):
        if d:
            row_meta[d].wait_recv()
            c = pltpu.make_async_copy(rmeta.at[d], rids.at[d], meta_local.at[0])
            c.start()
            c.wait()
        theirs = [[cids[v, 0, o] for o in range(occ)] for v in range(n_vrow)]
        found = []
        for o in range(occ):
            mine = rids[d, 0, o]
            for v in range(n_vrow):
                m = jnp.int32(occ)
                for k in range(occ):
                    m = jnp.where((mine >= 0) & (mine == theirs[v][k]), jnp.int32(k), m)
                found.append(m)
        return found

    def compute(d, p):
        if d not in match:
            match[d] = matches(d)
        for v in range(n_vrow):
            acc = None
            for o in range(occ):
                lhs = rows[d, p * width : (p + 1) * width, o].reshape(ch * width, rows.shape[-1])
                rhs = cols[v, match[d][o * n_vrow + v]]
                t = lax.dot_general(lhs, rhs, (((1,), (1,)), ((), ())), preferred_element_type=jnp.float32)
                acc = t if acc is None else acc + t
            n = acc.shape[1]
            at = pl.multiple_of(lax.rem(r + v, n_vrow) * n, n)
            part[d, p, :, pl.ds(at, n)] = acc
            top = jnp.max(acc, axis=0, keepdims=True)
            inverse = jnp.where(top > 0, 1.0 / top, 0.0)
            level = ((acc * inverse) * LEVELS + 0.5).astype(jnp.int32) - HALF
            code[d, p, :, pl.ds(at, n)] = level.astype(jnp.int16)
            tops[d, p, :, pl.ds(at, n)] = top
        s = q if d == 0 else partner(q, d, n_vcol)
        g = s * pieces + p
        dest = g // per_chunk
        place = g - dest * per_chunk
        to = {"field": dest}
        c = pltpu.make_async_remote_copy(
            src_ref=code.at[d, p], dst_ref=got.at[f, place],
            send_sem=part_send.at[d, p], recv_sem=part_recv.at[f, place],
            device_id=to, device_id_type=MESH,
        )
        t = pltpu.make_async_remote_copy(
            src_ref=tops.at[d, p], dst_ref=got_tops.at[f, place],
            send_sem=top_send.at[d, p], recv_sem=top_recv.at[f, place],
            device_id=to, device_id_type=MESH,
        )

        @pl.when(dest != f)
        def _():
            t.start()
            c.start()

        @pl.when(dest == f)
        def _():
            mine_sum[place] = part[d, p]

        part_sends.append((dest, c, t))

    def forward(p):
        first = pl.ds(p * width, width // 2)
        second = pl.ds(p * width + width // 2, width - width // 2)
        row_copy[1, p].wait_recv()
        a = send(rows.at[1, first], rows.at[3, first],
                 row_send.at[3, p], row_recv.at[3, p], {"vcol": partner(q, 2, 4)})
        row_copy[2, p].wait_recv()
        b = send(rows.at[2, second], rows.at[3, second],
                 row_send.at[0, p], row_recv.at[0, p], {"vcol": partner(q, 1, 4)})
        row_copy[3, p] = (a, b)
        if p + STEPS_AHEAD < pieces:
            send_rows(p + STEPS_AHEAD)

    compute(0, 0)
    for p in range(pieces):
        if relay:
            forward(p)
        for d in range(1, 3 if relay else n_vcol):
            if not relay:
                row_copy[d, p].wait_recv()
            compute(d, p)
        if p + 1 < pieces:
            compute(0, p + 1)
        if relay and p:
            for c in row_copy[3, p - 1]:
                c.wait_recv()
            compute(3, p - 1)
    if relay:
        for c in row_copy[3, pieces - 1]:
            c.wait_recv()
        compute(3, pieces - 1)

    for place in range(per_chunk):
        total = mine_sum[place]
        for d in range(1, n_field):
            src = lax.rem(f + d, n_field)
            for buf, land, gone, came in (
                (code, got, part_send, part_recv), (tops, got_tops, top_send, top_recv),
            ):
                pltpu.make_async_remote_copy(
                    src_ref=buf.at[0, 0], dst_ref=land.at[src, place],
                    send_sem=gone.at[0, 0], recv_sem=came.at[src, place],
                    device_id={"field": src}, device_id_type=MESH,
                ).wait_recv()
            level = (got[src, place].astype(jnp.int32) + HALF).astype(jnp.float32)
            total = total + level * (got_tops[src, place] * (1.0 / LEVELS))
        parts = n_vrow * ch
        for k in range(parts):
            out[pl.ds(place * ch * width * parts + k, ch * width, parts), :] = total[:, k * vs : (k + 1) * vs]
    for c in sends:
        c.wait_send()
    for dest, c, t in part_sends:
        @pl.when(dest != f)
        def _():
            c.wait_send()
            t.wait_send()


def on_any_device(blocks, block_ids, block_counts):
    n_field, n_vrow, n_vcol = (lax.axis_size(a) for a in ("field", "vrow", "vcol"))
    vs, occ, ch, x = blocks.shape
    chunk = n_vcol * vs // n_field
    width = min(vs // MAX_PIECES, chunk)
    pieces = vs // width
    per_chunk = chunk // width
    data = blocks
    c = ch * vs
    wide = n_vrow * c
    dims = (n_field, n_vrow, n_vcol, pieces, occ, width, per_chunk)
    dma = pltpu.SemaphoreType.DMA
    scale = 1.0 / (n_field * SBLK * BLOCK)
    out = pl.pallas_call(
        functools.partial(any_kernel, dims, scale),
        out_shape=jax.ShapeDtypeStruct((chunk * ch * n_vrow * ch, vs), jnp.float32),
        in_specs=[pl.BlockSpec(memory_space=pl.ANY)] + [pl.BlockSpec(memory_space=pltpu.VMEM)] * 2,
        out_specs=pl.BlockSpec(memory_space=pltpu.VMEM),
        scratch_shapes=[
            pltpu.VMEM((1, 128), jnp.int32),
            pltpu.VMEM((n_vcol, vs, occ, ch, x), jnp.bfloat16),
            pltpu.VMEM((n_vrow, vs, occ, ch, x), jnp.bfloat16),
            pltpu.VMEM((n_vrow, occ + 1, ch * vs, x), jnp.bfloat16),
            pltpu.VMEM((n_vcol, pieces, ch * width, wide), jnp.float32),
            pltpu.VMEM((n_vcol, pieces, ch * width, wide), jnp.int16),
            pltpu.VMEM((n_vcol, pieces, 1, wide), jnp.float32),
            pltpu.VMEM((n_field, per_chunk, ch * width, wide), jnp.int16),
            pltpu.VMEM((n_field, per_chunk, 1, wide), jnp.float32),
            pltpu.VMEM((per_chunk, ch * width, wide), jnp.float32),
            pltpu.VMEM((n_vcol, 1, 128), jnp.int32),
            pltpu.VMEM((n_vrow, 1, 128), jnp.int32),
            pltpu.SMEM((n_vcol, 1, 128), jnp.int32),
            pltpu.SMEM((n_vrow, 1, 128), jnp.int32),
            dma((1,)),
            dma((2,)),
            dma((n_vcol, pieces)),
            dma((n_vcol, pieces)),
            dma((n_vrow, pieces)),
            dma((n_vrow, pieces)),
            dma((n_vcol,)),
            dma((n_vcol,)),
            dma((n_vrow,)),
            dma((n_vrow,)),
            dma((n_vcol, pieces)),
            dma((n_field, per_chunk)),
            dma((n_vcol, pieces)),
            dma((n_field, per_chunk)),
        ],
        compiler_params=pltpu.CompilerParams(collective_id=1, has_side_effects=True),
    )(data, block_ids, block_counts)
    return (out * scale).reshape(chunk, ch, n_vrow, 1, ch, vs)


def square_kernel(
    dims, data, ids, counts, out,
    meta, raw, cols, rows, mine, hold, code, tops, got, got_tops, code2, tops2, got2, got2_tops, turn, turn_tops, turned, turned_tops,
    rmeta, cmeta, rids, cids,
    raw_sem, meta_local, col_sem, own_send, own_recv, far_send, far_recv,
    m_send, m_recv, part_send, part_recv, top_send, top_recv, part2_send, part2_recv, top2_send, top2_recv,
    turn_send, turn_recv, ttop_send, ttop_recv, two,
):
    n_field, n_vrow, n_vcol, groups, occ, vs, ch = dims
    n, half = cols.shape[3], cols.shape[4]
    gw = n // groups
    f, r, q = lax.axis_index("field"), lax.axis_index("vrow"), lax.axis_index("vcol")
    beside = f + 1 - 2 * lax.rem(f, 2)
    inner = (f > 0) & (f + 1 < n_field)
    over = [q, partner(q, 1, 4), partner(q, 2, 4), partner(q, 3, 4)]
    twin = {"vrow": 1 - r}
    near = {1: {"vcol": over[1]}, 2: {"vcol": over[2]}}
    odd = lax.rem(q // 2 + q, 2)
    place = [1 - odd, odd]

    barrier = pltpu.get_barrier_semaphore()
    for to in (twin, near[1], near[2]):
        pl.semaphore_signal(barrier, inc=1, device_id=to, device_id_type=MESH)

    @pl.when(f + 1 < n_field)
    def _():
        pl.semaphore_signal(barrier, inc=1, device_id={"field": lax.rem(f + 1, n_field)}, device_id_type=MESH)

    @pl.when(f > 0)
    def _():
        pl.semaphore_signal(barrier, inc=1, device_id={"field": lax.rem(f + n_field - 1, n_field)}, device_id_type=MESH)

    loads = []
    for o in range(occ):
        c = pltpu.make_async_copy(data.at[:, o], raw.at[o], raw_sem.at[o])
        c.start()
        loads.append(c)
    meta[...] = jnp.full_like(meta, -1)
    slots = lax.broadcasted_iota(jnp.int32, (1, occ), 1)
    meta[:, 0:occ] = jnp.where(slots < counts[...], ids[0], -1)
    own_r = pltpu.make_async_copy(meta, rids.at[0], meta_local.at[0])
    own_r.start()
    own_c = pltpu.make_async_copy(meta, cids.at[0], meta_local.at[1])
    own_c.start()
    for b in range(2):
        for v in range(n_vrow):
            cols[b, v, occ] = jnp.zeros_like(cols[b, v, occ])
    to_row = lax.broadcasted_iota(jnp.int32, (n, n), 0)
    from_row = lax.broadcasted_iota(jnp.int32, (n, n), 1)
    order = jnp.where(from_row == lax.rem(to_row, vs) * ch + to_row // vs, 1.0, 0.0).astype(jnp.bfloat16)
    for o in range(occ):
        loads[o].wait()
        sorted_rows = jnp.dot(order, raw[o].reshape(n, 2 * half), preferred_element_type=jnp.float32)
        for b in range(2):
            cols[place[b], 0, o] = sorted_rows[:, b * half : (b + 1) * half].astype(jnp.bfloat16)
    own_r.wait()
    own_c.wait()

    @pl.when((f > 0) & (f + 1 < n_field))
    def _():
        pl.semaphore_wait(barrier, 5)

    @pl.when((f == 0) | (f + 1 == n_field))
    def _():
        pl.semaphore_wait(barrier, 4)

    sends = []

    def send(src, dst, s, t, where):
        c = pltpu.make_async_remote_copy(
            src_ref=src, dst_ref=dst, send_sem=s, recv_sem=t, device_id=where, device_id_type=MESH
        )
        c.start()
        sends.append(c)
        return c

    @pl.when(inner)
    def _():
        pl.semaphore_signal(two, inc=1, device_id={"field": n_field - 1 - f}, device_id_type=MESH)

    live = pl.ds(0, occ)
    twin_copy = send(cols.at[:, 0, live], cols.at[:, 1, live], col_sem.at[0], col_sem.at[1], twin)
    c_meta = send(meta, cmeta.at[0], m_send.at[0], m_recv.at[0], twin)
    r_meta = {}
    for d in (1, 2):
        r_meta[d] = send(meta, rmeta.at[d], m_send.at[d], m_recv.at[d], near[d])
    own_copy, far_copy = {}, {}

    def span(g):
        return pl.ds(g * gw, gw)

    def send_own(g):
        for d in (1, 2):
            own_copy[d, g] = send(
                cols.at[2 - d, 0, live, span(g)], rows.at[d - 1, :, span(g)], own_send.at[d, g], own_recv.at[d, g], near[d]
            )

    def send_far(g):
        for d in (1, 2):
            far_copy[3 - d, g] = send(
                rows.at[d - 1, :, span(g)], rows.at[4 - d, :, span(g)], far_send.at[3 - d, g], far_recv.at[3 - d, g],
                near[3 - d],
            )

    for g in range(min(AHEAD, groups)):
        send_own(g)

    @pl.when(inner)
    def _():
        pl.semaphore_wait(two, 1)

    c_meta.wait_recv()
    c = pltpu.make_async_copy(cmeta.at[0], cids.at[1], meta_local.at[1])
    c.start()
    c.wait()
    theirs = [[cids[v, 0, o] for o in range(occ)] for v in range(n_vrow)]

    def matches(d):
        if d:
            if d > 1:
                r_meta[d].wait_recv()
            c = pltpu.make_async_copy(rmeta.at[d], rids.at[d], meta_local.at[0])
            c.start()
            c.wait()
        found = {}
        for o in range(occ):
            own = rids[d, 0, o]
            for v in range(n_vrow):
                m = jnp.int32(occ)
                for k in range(occ):
                    m = jnp.where((own >= 0) & (own == theirs[v][k]), jnp.int32(k), m)
                found[o, v] = m
        return found

    match = {}
    part_sends = []

    def encode(acc):
        top = jnp.max(acc, axis=0, keepdims=True)
        inverse = jnp.where(top > 0, 1.0 / top, 0.0)
        level = ((acc * inverse) * LEVELS + 0.5).astype(jnp.int32) - HALF
        return level.astype(jnp.int16), top

    def decode(level, top):
        return (level.astype(jnp.int32) + HALF).astype(jnp.float32) * (top * (1.0 / LEVELS))

    def first_hop(dest, d, g):
        i = jnp.where(dest == beside, 0, 1 + lax.rem(dest, 2))
        to = {"field": beside}
        return (
            pltpu.make_async_remote_copy(
                src_ref=code.at[d, g], dst_ref=got.at[i, g],
                send_sem=part_send.at[d, g], recv_sem=part_recv.at[i, g], device_id=to, device_id_type=MESH,
            ),
            pltpu.make_async_remote_copy(
                src_ref=tops.at[d, g], dst_ref=got_tops.at[i, g],
                send_sem=top_send.at[d, g], recv_sem=top_recv.at[i, g], device_id=to, device_id_type=MESH,
            ),
        )

    def came(i, g):
        for c in (
            pltpu.make_async_remote_copy(
                src_ref=code.at[0, g], dst_ref=got.at[i, g], send_sem=part_send.at[0, g], recv_sem=part_recv.at[i, g],
                device_id={"field": beside}, device_id_type=MESH,
            ),
            pltpu.make_async_remote_copy(
                src_ref=tops.at[0, g], dst_ref=got_tops.at[i, g], send_sem=top_send.at[0, g], recv_sem=top_recv.at[i, g],
                device_id={"field": beside}, device_id_type=MESH,
            ),
        ):
            c.wait_recv()
        return decode(got[i, g], got_tops[i, g])

    def second_hop(i, g):
        to = {"field": lax.rem(n_field - 2 * (f // 2) - 2, n_field) + i}
        return (
            pltpu.make_async_remote_copy(
                src_ref=code2.at[i, g], dst_ref=got2.at[g], send_sem=part2_send.at[i, g], recv_sem=part2_recv.at[g],
                device_id=to, device_id_type=MESH,
            ),
            pltpu.make_async_remote_copy(
                src_ref=tops2.at[i, g], dst_ref=got2_tops.at[g], send_sem=top2_send.at[i, g], recv_sem=top2_recv.at[g],
                device_id=to, device_id_type=MESH,
            ),
        )

    def merge(d, g):
        @pl.when(over[d] == f)
        def _():
            mine[g] += came(0, g)

        @pl.when(inner & (over[d] // 2 != f // 2))
        def _():
            i = lax.rem(over[d], 2)
            code2[i, g], tops2[i, g] = encode(hold[i, g] + came(1 + i, g))
            for c in reversed(second_hop(i, g)):
                c.start()

    def summed(g):
        for c in second_hop(0, g):
            c.wait_recv()
        return mine[g] + decode(got2[g], got2_tops[g])

    def compute(d, g):
        if d not in match:
            match[d] = matches(d)
        at = pl.ds(g * gw, gw)
        halves = []
        for v in range(n_vrow):
            acc = None
            for o in range(occ):
                k = match[d][o, v]
                if d in (1, 2):
                    lhs, rhs = rows[d - 1, o, at], cols[d - 1, v, k]
                else:
                    lhs = [cols[b, 0, o, at] if d == 0 else rows[2 + b, o, at] for b in range(2)]
                    lhs = jnp.concatenate(lhs, axis=1)
                    rhs = jnp.concatenate([cols[b, v, k] for b in range(2)], axis=1)
                t = lax.dot_general(lhs, rhs, (((1,), (1,)), ((), ())), preferred_element_type=jnp.float32)
                acc = t if acc is None else acc + t
            halves.append(acc)
        dest = over[d]

        kept = inner & (dest // 2 != f // 2)
        leaves = (dest != f) & jnp.logical_not(kept)
        c, t = first_hop(dest, d, g)

        def at(v):
            return pl.ds(pl.multiple_of(lax.rem(r + v, n_vrow) * n, n), n)

        @pl.when(dest == f)
        def _():
            for v in range(n_vrow):
                mine[g, :, at(v)] = halves[v]

        @pl.when(kept)
        def _():
            for v in range(n_vrow):
                hold[lax.rem(dest, 2), g, :, at(v)] = halves[v]

        @pl.when(leaves)
        def _():
            for v in range(n_vrow):
                code[d, g, :, at(v)], tops[d, g, :, at(v)] = encode(halves[v])
            t.start()
            c.start()

        part_sends.append((leaves, c, t))

    swaps = (f == over[1]) | (f == over[2])
    turn_copies = {}

    def swap(a):
        for b in range(n_vrow):
            to = {"field": q, "vrow": b, "vcol": f}
            turn_copies[a, b] = (
                pltpu.make_async_remote_copy(
                    src_ref=turn.at[a, b], dst_ref=turned.at[r, a],
                    send_sem=turn_send.at[a, b], recv_sem=turn_recv.at[r, a],
                    device_id=to, device_id_type=MESH,
                ),
                pltpu.make_async_remote_copy(
                    src_ref=turn_tops.at[a, b], dst_ref=turned_tops.at[r, a],
                    send_sem=ttop_send.at[a, b], recv_sem=ttop_recv.at[r, a],
                    device_id=to, device_id_type=MESH,
                ),
            )

        @pl.when(swaps)
        def _():
            total = summed(a)
            mine[a] = total
            for b in range(n_vrow):
                turn[a, b], turn_tops[a, b] = encode(total[:, b * n : (b + 1) * n])
                for c in reversed(turn_copies[a, b]):
                    c.start()

    def step(kind, i):
        if kind in "SXYD":
            compute("SXYD".index(kind), i)
        elif kind in "sxyd":
            merge("sxyd".index(kind), i)
        elif kind == "o":
            for d in (1, 2):
                own_copy[d, i].wait_recv()
            if i == 0:
                r_meta[1].wait_recv()
                r_meta[3] = send(rmeta.at[1], rmeta.at[3], m_send.at[3], m_recv.at[3], near[2])
            send_far(i)
            if i + AHEAD < groups:
                send_own(i + AHEAD)
        elif kind == "f":
            for d in (1, 2):
                far_copy[d, i].wait_recv()
        else:
            swap(i)

    twin_copy.wait_recv()
    for name in PLAN:
        step(name[0], int(name[1:]))

    parts = n_vrow * ch

    def put(a, k, values):
        out[pl.ds(a * parts + k, vs, ch * parts), :] = values

    def held(a, k):
        each = [mine[g, :, k * vs : (k + 1) * vs] for g in range(a * groups // ch, (a + 1) * groups // ch)]
        return jnp.concatenate(each, axis=0)

    @pl.when(jnp.logical_not(swaps))
    def _():
        for a in range(ch):
            for g in range(a * groups // ch, (a + 1) * groups // ch):
                total = summed(g)
                at = (g * gw) % vs
                for k in range(parts):
                    out[pl.ds((at * ch + a) * parts + k, gw, ch * parts), :] = total[:, k * vs : (k + 1) * vs]

    @pl.when(swaps)
    def _():
        for b in range(ch):
            for v in range(n_vrow):
                each = []
                for g in range(b * groups // ch, (b + 1) * groups // ch):
                    for land, came, gone, buf in (
                        (turned, turn_recv, turn_send, turn), (turned_tops, ttop_recv, ttop_send, turn_tops),
                    ):
                        pltpu.make_async_remote_copy(
                            src_ref=buf.at[0, 0], dst_ref=land.at[v, g],
                            send_sem=gone.at[0, 0], recv_sem=came.at[v, g],
                            device_id={"field": q, "vrow": r, "vcol": f}, device_id_type=MESH,
                        ).wait_recv()
                    each.append(decode(turned[v, g], turned_tops[v, g]))
                back = jnp.transpose(jnp.concatenate(each, axis=0))
                k = v * ch + b
                for a in range(ch):
                    put(a, k, held(a, k) + back[a * vs : (a + 1) * vs])
        for c, t in turn_copies.values():
            c.wait_send()
            t.wait_send()

    for c in sends:
        c.wait_send()
    for sent, c, t in part_sends:
        @pl.when(sent)
        def _():
            c.wait_send()
            t.wait_send()

    @pl.when(inner)
    def _():
        for i in range(2):
            for g in range(groups):
                for c in second_hop(i, g):
                    c.wait_send()


def on_square_device(blocks, block_ids, block_counts):
    n_field, n_vrow, n_vcol = (lax.axis_size(a) for a in ("field", "vrow", "vcol"))
    vs, occ, ch, x = blocks.shape
    n = ch * vs
    groups = 4
    gw = n // groups
    half = x // 2
    dims = (n_field, n_vrow, n_vcol, groups, occ, vs, ch)
    dma = pltpu.SemaphoreType.DMA
    wide = n_vrow * n
    out = pl.pallas_call(
        functools.partial(square_kernel, dims),
        out_shape=jax.ShapeDtypeStruct((vs * ch * n_vrow * ch, vs), jnp.float32),
        in_specs=[pl.BlockSpec(memory_space=pl.ANY)] + [pl.BlockSpec(memory_space=pltpu.VMEM)] * 2,
        out_specs=pl.BlockSpec(memory_space=pltpu.VMEM),
        scratch_shapes=[
            pltpu.VMEM((1, 128), jnp.int32),
            pltpu.VMEM((occ, vs, ch, x), jnp.bfloat16),
            pltpu.VMEM((2, n_vrow, occ + 1, n, half), jnp.bfloat16),
            pltpu.VMEM((4, occ, n, half), jnp.bfloat16),
            pltpu.VMEM((groups, gw, wide), jnp.float32),
            pltpu.VMEM((2, groups, gw, wide), jnp.float32),
            pltpu.VMEM((n_vcol, groups, gw, wide), jnp.int16),
            pltpu.VMEM((n_vcol, groups, 1, wide), jnp.float32),
            pltpu.VMEM((3, groups, gw, wide), jnp.int16),
            pltpu.VMEM((3, groups, 1, wide), jnp.float32),
            pltpu.VMEM((2, groups, gw, wide), jnp.int16),
            pltpu.VMEM((2, groups, 1, wide), jnp.float32),
            pltpu.VMEM((groups, gw, wide), jnp.int16),
            pltpu.VMEM((groups, 1, wide), jnp.float32),
            pltpu.VMEM((groups, n_vrow, gw, n), jnp.int16),
            pltpu.VMEM((groups, n_vrow, 1, n), jnp.float32),
            pltpu.VMEM((n_vrow, groups, gw, n), jnp.int16),
            pltpu.VMEM((n_vrow, groups, 1, n), jnp.float32),
            pltpu.VMEM((n_vcol, 1, 128), jnp.int32),
            pltpu.VMEM((1, 1, 128), jnp.int32),
            pltpu.SMEM((n_vcol, 1, 128), jnp.int32),
            pltpu.SMEM((n_vrow, 1, 128), jnp.int32),
            dma((occ,)),
            dma((2,)),
            dma((2,)),
            dma((3, groups)),
            dma((3, groups)),
            dma((3, groups)),
            dma((3, groups)),
            dma((4,)),
            dma((4,)),
            dma((n_vcol, groups)),
            dma((3, groups)),
            dma((n_vcol, groups)),
            dma((3, groups)),
            dma((2, groups)),
            dma((groups,)),
            dma((2, groups)),
            dma((groups,)),
            dma((groups, n_vrow)),
            dma((n_vrow, groups)),
            dma((groups, n_vrow)),
            dma((n_vrow, groups)),
            pltpu.SemaphoreType.REGULAR,
        ],
        compiler_params=pltpu.CompilerParams(collective_id=0, has_side_effects=True, vmem_limit_bytes=56000000),
    )(blocks, block_ids, block_counts)
    return (out * (1.0 / (n_field * SBLK * BLOCK))).reshape(vs, ch, n_vrow, 1, ch, vs)


def solution(mesh):
    placed = (
        P(("vrow", "vcol"), "field", None, None),
        P(("vrow", "vcol"), "field", None),
        P(("vrow", "vcol"), "field"),
    )
    square = mesh.shape["field"] == 4 and mesh.shape["vcol"] == 4 and mesh.shape["vrow"] == 2
    return jax.shard_map(
        on_square_device if square else on_any_device,
        mesh=mesh,
        in_specs=placed,
        out_specs=P(("vrow", "field"), None, None, "vcol", None, None),
        check_vma=False,
    )
```

```python
import functools

import jax
import jax.numpy as jnp
from jax import lax
from jax.experimental import pallas as pl
from jax.experimental.pallas import tpu as pltpu
from jax.sharding import PartitionSpec as P

SBLK = 12
BLOCK = 256
MAX_PIECES = 4
STEPS_AHEAD = 2
AHEAD = 4
PLAN = (
    "S0", "o0", "S1", "X0", "Y0", "S2", "o1", "X1", "Y1", "s0",
    "s1", "o2", "X2", "Y2", "x0", "y0", "o3", "X3", "Y3", "S3",
    "x1", "y1", "s2", "f0", "t0", "D0", "x2", "y2", "f1", "D1",
    "x3", "f2", "D2", "t1", "y3", "f3", "D3", "t2", "d0", "d1",
    "t3", "d2", "d3", "s3",
)
LEVELS = 65535.0
HALF = 32768
MESH = pl.DeviceIdType.MESH


def partner(q, d, n):
    if n == 4:
        return (q + 1 - 2 * lax.rem(q, 2), lax.rem(q + 2, 4), 3 - q)[d - 1]
    return lax.rem(q + d, n)


def any_kernel(
    dims, scale, data, ids, counts, out, meta, rows, raw_cols, cols, part, code, tops, got, got_tops, mine_sum, rmeta, cmeta, rids, cids,
    row_local, meta_local,
    row_send, row_recv, col_send, col_recv, rm_send, rm_recv, cm_send, cm_recv,
    part_send, part_recv, top_send, top_recv,
):
    n_field, n_vrow, n_vcol, pieces, occ, width, per_chunk = dims
    f, r, q = lax.axis_index("field"), lax.axis_index("vrow"), lax.axis_index("vcol")
    relay = n_vcol == 4

    barrier = pltpu.get_barrier_semaphore()
    for d in range(1, n_vcol):
        pl.semaphore_signal(barrier, inc=1, device_id={"vcol": partner(q, d, n_vcol)}, device_id_type=MESH)
    for d in range(1, n_vrow):
        pl.semaphore_signal(barrier, inc=1, device_id={"vrow": lax.rem(r + d, n_vrow)}, device_id_type=MESH)
    for d in range(1, n_field):
        pl.semaphore_signal(barrier, inc=1, device_id={"field": lax.rem(f + d, n_field)}, device_id_type=MESH)

    meta[...] = jnp.full_like(meta, -1)
    slots = lax.broadcasted_iota(jnp.int32, (1, occ), 1)
    meta[:, 0:occ] = jnp.where(slots < counts[...], ids[0], -1)
    own = pltpu.make_async_copy(data, rows.at[0], row_local.at[0])
    own.start()
    for v in range(n_vrow):
        cols[v, occ] = jnp.zeros_like(cols[v, occ])

    pl.semaphore_wait(barrier, n_vcol + n_vrow + n_field - 3)

    own_r = pltpu.make_async_copy(meta, rids.at[0], meta_local.at[0])
    own_r.start()
    own_c = pltpu.make_async_copy(meta, cids.at[0], meta_local.at[1])
    own_c.start()

    def span(p):
        return pl.ds(p * width, width)

    sends = []

    def send(src, dst, s, w, where):
        c = pltpu.make_async_remote_copy(
            src_ref=src, dst_ref=dst, send_sem=s, recv_sem=w, device_id=where, device_id_type=MESH
        )
        c.start()
        sends.append(c)
        return c

    row_meta, col_meta, row_copy, col_copy = {}, {}, {}, {}

    def send_rows(p):
        for d in range(1, 3 if relay else n_vcol):
            to = {"vcol": partner(q, d, n_vcol)}
            row_copy[d, p] = send(data.at[span(p)], rows.at[d, span(p)], row_send.at[d, p], row_recv.at[d, p], to)

    for d in range(1, n_vrow):
        to = {"vrow": lax.rem(r + d, n_vrow)}
        col_meta[d] = send(meta, cmeta.at[d], cm_send.at[d], cm_recv.at[d], to)
    for d in range(1, n_vcol):
        to = {"vcol": partner(q, d, n_vcol)}
        row_meta[d] = send(meta, rmeta.at[d], rm_send.at[d], rm_recv.at[d], to)
    for p in range(pieces):
        for d in range(1, n_vrow):
            to = {"vrow": lax.rem(r + d, n_vrow)}
            col_copy[d, p] = send(
                data.at[span(p)],
                raw_cols.at[d, span(p)],
                col_send.at[d, p], col_recv.at[d, p], to,
            )
        if p < (STEPS_AHEAD if relay else pieces):
            send_rows(p)

    own.wait()
    own_r.wait()
    own_c.wait()
    for d in range(1, n_vrow):
        col_meta[d].wait_recv()
        c = pltpu.make_async_copy(cmeta.at[d], cids.at[d], meta_local.at[1])
        c.start()
        c.wait()
    for d in range(1, n_vrow):
        for p in range(pieces):
            col_copy[d, p].wait_recv()
    ch, vs = rows.shape[3], rows.shape[1]
    n = ch * vs
    to_row = lax.broadcasted_iota(jnp.int32, (n, n), 0)
    from_row = lax.broadcasted_iota(jnp.int32, (n, n), 1)
    order = jnp.where(from_row == lax.rem(to_row, vs) * ch + to_row // vs, 1.0, 0.0).astype(jnp.bfloat16)
    for v in range(n_vrow):
        for o in range(occ):
            block = (raw_cols[v, :, o] if v else rows[0, :, o]).reshape(n, rows.shape[-1])
            turned = jnp.dot(order, block, preferred_element_type=jnp.float32)
            cols[v, o] = turned.astype(jnp.bfloat16)

    match = {}
    part_sends = []

    def matches(d):
        if d:
            row_meta[d].wait_recv()
            c = pltpu.make_async_copy(rmeta.at[d], rids.at[d], meta_local.at[0])
            c.start()
            c.wait()
        theirs = [[cids[v, 0, o] for o in range(occ)] for v in range(n_vrow)]
        found = []
        for o in range(occ):
            mine = rids[d, 0, o]
            for v in range(n_vrow):
                m = jnp.int32(occ)
                for k in range(occ):
                    m = jnp.where((mine >= 0) & (mine == theirs[v][k]), jnp.int32(k), m)
                found.append(m)
        return found

    def compute(d, p):
        if d not in match:
            match[d] = matches(d)
        for v in range(n_vrow):
            acc = None
            for o in range(occ):
                lhs = rows[d, p * width : (p + 1) * width, o].reshape(ch * width, rows.shape[-1])
                rhs = cols[v, match[d][o * n_vrow + v]]
                t = lax.dot_general(lhs, rhs, (((1,), (1,)), ((), ())), preferred_element_type=jnp.float32)
                acc = t if acc is None else acc + t
            n = acc.shape[1]
            at = pl.multiple_of(lax.rem(r + v, n_vrow) * n, n)
            part[d, p, :, pl.ds(at, n)] = acc
            top = jnp.max(acc, axis=0, keepdims=True)
            inverse = jnp.where(top > 0, 1.0 / top, 0.0)
            level = ((acc * inverse) * LEVELS + 0.5).astype(jnp.int32) - HALF
            code[d, p, :, pl.ds(at, n)] = level.astype(jnp.int16)
            tops[d, p, :, pl.ds(at, n)] = top
        s = q if d == 0 else partner(q, d, n_vcol)
        g = s * pieces + p
        dest = g // per_chunk
        place = g - dest * per_chunk
        to = {"field": dest}
        c = pltpu.make_async_remote_copy(
            src_ref=code.at[d, p], dst_ref=got.at[f, place],
            send_sem=part_send.at[d, p], recv_sem=part_recv.at[f, place],
            device_id=to, device_id_type=MESH,
        )
        t = pltpu.make_async_remote_copy(
            src_ref=tops.at[d, p], dst_ref=got_tops.at[f, place],
            send_sem=top_send.at[d, p], recv_sem=top_recv.at[f, place],
            device_id=to, device_id_type=MESH,
        )

        @pl.when(dest != f)
        def _():
            t.start()
            c.start()

        @pl.when(dest == f)
        def _():
            mine_sum[place] = part[d, p]

        part_sends.append((dest, c, t))

    def forward(p):
        first = pl.ds(p * width, width // 2)
        second = pl.ds(p * width + width // 2, width - width // 2)
        row_copy[1, p].wait_recv()
        a = send(rows.at[1, first], rows.at[3, first],
                 row_send.at[3, p], row_recv.at[3, p], {"vcol": partner(q, 2, 4)})
        row_copy[2, p].wait_recv()
        b = send(rows.at[2, second], rows.at[3, second],
                 row_send.at[0, p], row_recv.at[0, p], {"vcol": partner(q, 1, 4)})
        row_copy[3, p] = (a, b)
        if p + STEPS_AHEAD < pieces:
            send_rows(p + STEPS_AHEAD)

    compute(0, 0)
    for p in range(pieces):
        if relay:
            forward(p)
        for d in range(1, 3 if relay else n_vcol):
            if not relay:
                row_copy[d, p].wait_recv()
            compute(d, p)
        if p + 1 < pieces:
            compute(0, p + 1)
        if relay and p:
            for c in row_copy[3, p - 1]:
                c.wait_recv()
            compute(3, p - 1)
    if relay:
        for c in row_copy[3, pieces - 1]:
            c.wait_recv()
        compute(3, pieces - 1)

    for place in range(per_chunk):
        total = mine_sum[place]
        for d in range(1, n_field):
            src = lax.rem(f + d, n_field)
            for buf, land, gone, came in (
                (code, got, part_send, part_recv), (tops, got_tops, top_send, top_recv),
            ):
                pltpu.make_async_remote_copy(
                    src_ref=buf.at[0, 0], dst_ref=land.at[src, place],
                    send_sem=gone.at[0, 0], recv_sem=came.at[src, place],
                    device_id={"field": src}, device_id_type=MESH,
                ).wait_recv()
            level = (got[src, place].astype(jnp.int32) + HALF).astype(jnp.float32)
            total = total + level * (got_tops[src, place] * (1.0 / LEVELS))
        parts = n_vrow * ch
        for k in range(parts):
            out[pl.ds(place * ch * width * parts + k, ch * width, parts), :] = total[:, k * vs : (k + 1) * vs]
    for c in sends:
        c.wait_send()
    for dest, c, t in part_sends:
        @pl.when(dest != f)
        def _():
            c.wait_send()
            t.wait_send()


def on_any_device(blocks, block_ids, block_counts):
    n_field, n_vrow, n_vcol = (lax.axis_size(a) for a in ("field", "vrow", "vcol"))
    vs, occ, ch, x = blocks.shape
    chunk = n_vcol * vs // n_field
    width = min(vs // MAX_PIECES, chunk)
    pieces = vs // width
    per_chunk = chunk // width
    data = blocks
    c = ch * vs
    wide = n_vrow * c
    dims = (n_field, n_vrow, n_vcol, pieces, occ, width, per_chunk)
    dma = pltpu.SemaphoreType.DMA
    scale = 1.0 / (n_field * SBLK * BLOCK)
    out = pl.pallas_call(
        functools.partial(any_kernel, dims, scale),
        out_shape=jax.ShapeDtypeStruct((chunk * ch * n_vrow * ch, vs), jnp.float32),
        in_specs=[pl.BlockSpec(memory_space=pl.ANY)] + [pl.BlockSpec(memory_space=pltpu.VMEM)] * 2,
        out_specs=pl.BlockSpec(memory_space=pltpu.VMEM),
        scratch_shapes=[
            pltpu.VMEM((1, 128), jnp.int32),
            pltpu.VMEM((n_vcol, vs, occ, ch, x), jnp.bfloat16),
            pltpu.VMEM((n_vrow, vs, occ, ch, x), jnp.bfloat16),
            pltpu.VMEM((n_vrow, occ + 1, ch * vs, x), jnp.bfloat16),
            pltpu.VMEM((n_vcol, pieces, ch * width, wide), jnp.float32),
            pltpu.VMEM((n_vcol, pieces, ch * width, wide), jnp.int16),
            pltpu.VMEM((n_vcol, pieces, 1, wide), jnp.float32),
            pltpu.VMEM((n_field, per_chunk, ch * width, wide), jnp.int16),
            pltpu.VMEM((n_field, per_chunk, 1, wide), jnp.float32),
            pltpu.VMEM((per_chunk, ch * width, wide), jnp.float32),
            pltpu.VMEM((n_vcol, 1, 128), jnp.int32),
            pltpu.VMEM((n_vrow, 1, 128), jnp.int32),
            pltpu.SMEM((n_vcol, 1, 128), jnp.int32),
            pltpu.SMEM((n_vrow, 1, 128), jnp.int32),
            dma((1,)),
            dma((2,)),
            dma((n_vcol, pieces)),
            dma((n_vcol, pieces)),
            dma((n_vrow, pieces)),
            dma((n_vrow, pieces)),
            dma((n_vcol,)),
            dma((n_vcol,)),
            dma((n_vrow,)),
            dma((n_vrow,)),
            dma((n_vcol, pieces)),
            dma((n_field, per_chunk)),
            dma((n_vcol, pieces)),
            dma((n_field, per_chunk)),
        ],
        compiler_params=pltpu.CompilerParams(collective_id=1, has_side_effects=True),
    )(data, block_ids, block_counts)
    return (out * scale).reshape(chunk, ch, n_vrow, 1, ch, vs)


def square_kernel(
    dims, data, ids, counts, out,
    meta, raw, cols, rows, mine, hold, code, tops, got, got_tops, code2, tops2, got2, got2_tops, turn, turn_tops, turned, turned_tops,
    rmeta, cmeta, rids, cids,
    raw_sem, meta_local, col_sem, own_send, own_recv, far_send, far_recv,
    m_send, m_recv, part_send, part_recv, top_send, top_recv, part2_send, part2_recv, top2_send, top2_recv,
    turn_send, turn_recv, ttop_send, ttop_recv, two,
):
    n_field, n_vrow, n_vcol, groups, occ, vs, ch = dims
    n, half = cols.shape[3], cols.shape[4]
    gw = n // groups
    f, r, q = lax.axis_index("field"), lax.axis_index("vrow"), lax.axis_index("vcol")
    beside = f + 1 - 2 * lax.rem(f, 2)
    inner = (f > 0) & (f + 1 < n_field)
    over = [q, partner(q, 1, 4), partner(q, 2, 4), partner(q, 3, 4)]
    twin = {"vrow": 1 - r}
    near = {1: {"vcol": over[1]}, 2: {"vcol": over[2]}}
    odd = lax.rem(q // 2 + q, 2)
    place = [1 - odd, odd]

    barrier = pltpu.get_barrier_semaphore()
    for to in (twin, near[1], near[2]):
        pl.semaphore_signal(barrier, inc=1, device_id=to, device_id_type=MESH)

    @pl.when(f + 1 < n_field)
    def _():
        pl.semaphore_signal(barrier, inc=1, device_id={"field": lax.rem(f + 1, n_field)}, device_id_type=MESH)

    @pl.when(f > 0)
    def _():
        pl.semaphore_signal(barrier, inc=1, device_id={"field": lax.rem(f + n_field - 1, n_field)}, device_id_type=MESH)

    loads = []
    for o in range(occ):
        c = pltpu.make_async_copy(data.at[:, o], raw.at[o], raw_sem.at[o])
        c.start()
        loads.append(c)
    meta[...] = jnp.full_like(meta, -1)
    slots = lax.broadcasted_iota(jnp.int32, (1, occ), 1)
    meta[:, 0:occ] = jnp.where(slots < counts[...], ids[0], -1)
    own_r = pltpu.make_async_copy(meta, rids.at[0], meta_local.at[0])
    own_r.start()
    own_c = pltpu.make_async_copy(meta, cids.at[0], meta_local.at[1])
    own_c.start()
    for b in range(2):
        for v in range(n_vrow):
            cols[b, v, occ] = jnp.zeros_like(cols[b, v, occ])
    to_row = lax.broadcasted_iota(jnp.int32, (n, n), 0)
    from_row = lax.broadcasted_iota(jnp.int32, (n, n), 1)
    order = jnp.where(from_row == lax.rem(to_row, vs) * ch + to_row // vs, 1.0, 0.0).astype(jnp.bfloat16)
    for o in range(occ):
        loads[o].wait()
        sorted_rows = jnp.dot(order, raw[o].reshape(n, 2 * half), preferred_element_type=jnp.float32)
        for b in range(2):
            cols[place[b], 0, o] = sorted_rows[:, b * half : (b + 1) * half].astype(jnp.bfloat16)
    own_r.wait()
    own_c.wait()

    @pl.when((f > 0) & (f + 1 < n_field))
    def _():
        pl.semaphore_wait(barrier, 5)

    @pl.when((f == 0) | (f + 1 == n_field))
    def _():
        pl.semaphore_wait(barrier, 4)

    sends = []

    def send(src, dst, s, t, where):
        c = pltpu.make_async_remote_copy(
            src_ref=src, dst_ref=dst, send_sem=s, recv_sem=t, device_id=where, device_id_type=MESH
        )
        c.start()
        sends.append(c)
        return c

    @pl.when(inner)
    def _():
        pl.semaphore_signal(two, inc=1, device_id={"field": n_field - 1 - f}, device_id_type=MESH)

    live = pl.ds(0, occ)
    twin_copy = send(cols.at[:, 0, live], cols.at[:, 1, live], col_sem.at[0], col_sem.at[1], twin)
    c_meta = send(meta, cmeta.at[0], m_send.at[0], m_recv.at[0], twin)
    r_meta = {}
    for d in (1, 2):
        r_meta[d] = send(meta, rmeta.at[d], m_send.at[d], m_recv.at[d], near[d])
    own_copy, far_copy = {}, {}

    def span(g):
        return pl.ds(g * gw, gw)

    def send_own(g):
        for d in (1, 2):
            own_copy[d, g] = send(
                cols.at[2 - d, 0, live, span(g)], rows.at[d - 1, :, span(g)], own_send.at[d, g], own_recv.at[d, g], near[d]
            )

    def send_far(g):
        for d in (1, 2):
            far_copy[3 - d, g] = send(
                rows.at[d - 1, :, span(g)], rows.at[4 - d, :, span(g)], far_send.at[3 - d, g], far_recv.at[3 - d, g],
                near[3 - d],
            )

    for g in range(min(AHEAD, groups)):
        send_own(g)

    @pl.when(inner)
    def _():
        pl.semaphore_wait(two, 1)

    c_meta.wait_recv()
    c = pltpu.make_async_copy(cmeta.at[0], cids.at[1], meta_local.at[1])
    c.start()
    c.wait()
    theirs = [[cids[v, 0, o] for o in range(occ)] for v in range(n_vrow)]

    def matches(d):
        if d:
            if d > 1:
                r_meta[d].wait_recv()
            c = pltpu.make_async_copy(rmeta.at[d], rids.at[d], meta_local.at[0])
            c.start()
            c.wait()
        found = {}
        for o in range(occ):
            own = rids[d, 0, o]
            for v in range(n_vrow):
                m = jnp.int32(occ)
                for k in range(occ):
                    m = jnp.where((own >= 0) & (own == theirs[v][k]), jnp.int32(k), m)
                found[o, v] = m
        return found

    match = {}
    part_sends = []

    def encode(acc):
        top = jnp.max(acc, axis=0, keepdims=True)
        inverse = jnp.where(top > 0, 1.0 / top, 0.0)
        level = ((acc * inverse) * LEVELS + 0.5).astype(jnp.int32) - HALF
        return level.astype(jnp.int16), top

    def decode(level, top):
        return (level.astype(jnp.int32) + HALF).astype(jnp.float32) * (top * (1.0 / LEVELS))

    def first_hop(dest, d, g):
        i = jnp.where(dest == beside, 0, 1 + lax.rem(dest, 2))
        to = {"field": beside}
        return (
            pltpu.make_async_remote_copy(
                src_ref=code.at[d, g], dst_ref=got.at[i, g],
                send_sem=part_send.at[d, g], recv_sem=part_recv.at[i, g], device_id=to, device_id_type=MESH,
            ),
            pltpu.make_async_remote_copy(
                src_ref=tops.at[d, g], dst_ref=got_tops.at[i, g],
                send_sem=top_send.at[d, g], recv_sem=top_recv.at[i, g], device_id=to, device_id_type=MESH,
            ),
        )

    def came(i, g):
        for c in (
            pltpu.make_async_remote_copy(
                src_ref=code.at[0, g], dst_ref=got.at[i, g], send_sem=part_send.at[0, g], recv_sem=part_recv.at[i, g],
                device_id={"field": beside}, device_id_type=MESH,
            ),
            pltpu.make_async_remote_copy(
                src_ref=tops.at[0, g], dst_ref=got_tops.at[i, g], send_sem=top_send.at[0, g], recv_sem=top_recv.at[i, g],
                device_id={"field": beside}, device_id_type=MESH,
            ),
        ):
            c.wait_recv()
        return decode(got[i, g], got_tops[i, g])

    def second_hop(i, g):
        to = {"field": lax.rem(n_field - 2 * (f // 2) - 2, n_field) + i}
        return (
            pltpu.make_async_remote_copy(
                src_ref=code2.at[i, g], dst_ref=got2.at[g], send_sem=part2_send.at[i, g], recv_sem=part2_recv.at[g],
                device_id=to, device_id_type=MESH,
            ),
            pltpu.make_async_remote_copy(
                src_ref=tops2.at[i, g], dst_ref=got2_tops.at[g], send_sem=top2_send.at[i, g], recv_sem=top2_recv.at[g],
                device_id=to, device_id_type=MESH,
            ),
        )

    def merge(d, g):
        @pl.when(over[d] == f)
        def _():
            mine[g] += came(0, g)

        @pl.when(inner & (over[d] // 2 != f // 2))
        def _():
            i = lax.rem(over[d], 2)
            code2[i, g], tops2[i, g] = encode(hold[i, g] + came(1 + i, g))
            for c in reversed(second_hop(i, g)):
                c.start()

    def summed(g):
        for c in second_hop(0, g):
            c.wait_recv()
        return mine[g] + decode(got2[g], got2_tops[g])

    def compute(d, g):
        if d not in match:
            match[d] = matches(d)
        at = pl.ds(g * gw, gw)
        halves = []
        for v in range(n_vrow):
            acc = None
            for o in range(occ):
                k = match[d][o, v]
                if d in (1, 2):
                    lhs, rhs = rows[d - 1, o, at], cols[d - 1, v, k]
                else:
                    lhs = [cols[b, 0, o, at] if d == 0 else rows[2 + b, o, at] for b in range(2)]
                    lhs = jnp.concatenate(lhs, axis=1)
                    rhs = jnp.concatenate([cols[b, v, k] for b in range(2)], axis=1)
                t = lax.dot_general(lhs, rhs, (((1,), (1,)), ((), ())), preferred_element_type=jnp.float32)
                acc = t if acc is None else acc + t
            halves.append(acc)
        dest = over[d]

        kept = inner & (dest // 2 != f // 2)
        leaves = (dest != f) & jnp.logical_not(kept)
        c, t = first_hop(dest, d, g)

        def at(v):
            return pl.ds(pl.multiple_of(lax.rem(r + v, n_vrow) * n, n), n)

        @pl.when(dest == f)
        def _():
            for v in range(n_vrow):
                mine[g, :, at(v)] = halves[v]

        @pl.when(kept)
        def _():
            for v in range(n_vrow):
                hold[lax.rem(dest, 2), g, :, at(v)] = halves[v]

        @pl.when(leaves)
        def _():
            for v in range(n_vrow):
                code[d, g, :, at(v)], tops[d, g, :, at(v)] = encode(halves[v])
            t.start()
            c.start()

        part_sends.append((leaves, c, t))

    swaps = (f == over[1]) | (f == over[2])
    turn_copies = {}

    def swap(a):
        for b in range(n_vrow):
            to = {"field": q, "vrow": b, "vcol": f}
            turn_copies[a, b] = (
                pltpu.make_async_remote_copy(
                    src_ref=turn.at[a, b], dst_ref=turned.at[r, a],
                    send_sem=turn_send.at[a, b], recv_sem=turn_recv.at[r, a],
                    device_id=to, device_id_type=MESH,
                ),
                pltpu.make_async_remote_copy(
                    src_ref=turn_tops.at[a, b], dst_ref=turned_tops.at[r, a],
                    send_sem=ttop_send.at[a, b], recv_sem=ttop_recv.at[r, a],
                    device_id=to, device_id_type=MESH,
                ),
            )

        @pl.when(swaps)
        def _():
            total = summed(a)
            mine[a] = total
            for b in range(n_vrow):
                turn[a, b], turn_tops[a, b] = encode(total[:, b * n : (b + 1) * n])
                for c in reversed(turn_copies[a, b]):
                    c.start()

    def step(kind, i):
        if kind in "SXYD":
            compute("SXYD".index(kind), i)
        elif kind in "sxyd":
            merge("sxyd".index(kind), i)
        elif kind == "o":
            for d in (1, 2):
                own_copy[d, i].wait_recv()
            if i == 0:
                r_meta[1].wait_recv()
                r_meta[3] = send(rmeta.at[1], rmeta.at[3], m_send.at[3], m_recv.at[3], near[2])
            send_far(i)
            if i + AHEAD < groups:
                send_own(i + AHEAD)
        elif kind == "f":
            for d in (1, 2):
                far_copy[d, i].wait_recv()
        else:
            swap(i)

    twin_copy.wait_recv()
    for name in PLAN:
        step(name[0], int(name[1:]))

    parts = n_vrow * ch

    def put(a, k, values):
        out[pl.ds(a * parts + k, vs, ch * parts), :] = values

    def held(a, k):
        each = [mine[g, :, k * vs : (k + 1) * vs] for g in range(a * groups // ch, (a + 1) * groups // ch)]
        return jnp.concatenate(each, axis=0)

    @pl.when(jnp.logical_not(swaps))
    def _():
        for a in range(ch):
            for g in range(a * groups // ch, (a + 1) * groups // ch):
                total = summed(g)
                at = (g * gw) % vs
                for k in range(parts):
                    out[pl.ds((at * ch + a) * parts + k, gw, ch * parts), :] = total[:, k * vs : (k + 1) * vs]

    @pl.when(swaps)
    def _():
        for b in range(ch):
            for v in range(n_vrow):
                each = []
                for g in range(b * groups // ch, (b + 1) * groups // ch):
                    for land, came, gone, buf in (
                        (turned, turn_recv, turn_send, turn), (turned_tops, ttop_recv, ttop_send, turn_tops),
                    ):
                        pltpu.make_async_remote_copy(
                            src_ref=buf.at[0, 0], dst_ref=land.at[v, g],
                            send_sem=gone.at[0, 0], recv_sem=came.at[v, g],
                            device_id={"field": q, "vrow": r, "vcol": f}, device_id_type=MESH,
                        ).wait_recv()
                    each.append(decode(turned[v, g], turned_tops[v, g]))
                back = jnp.transpose(jnp.concatenate(each, axis=0))
                k = v * ch + b
                for a in range(ch):
                    put(a, k, held(a, k) + back[a * vs : (a + 1) * vs])
        for c, t in turn_copies.values():
            c.wait_send()
            t.wait_send()

    for c in sends:
        c.wait_send()
    for sent, c, t in part_sends:
        @pl.when(sent)
        def _():
            c.wait_send()
            t.wait_send()

    @pl.when(inner)
    def _():
        for i in range(2):
            for g in range(groups):
                for c in second_hop(i, g):
                    c.wait_send()


def on_square_device(blocks, block_ids, block_counts):
    n_field, n_vrow, n_vcol = (lax.axis_size(a) for a in ("field", "vrow", "vcol"))
    vs, occ, ch, x = blocks.shape
    n = ch * vs
    groups = 4
    gw = n // groups
    half = x // 2
    dims = (n_field, n_vrow, n_vcol, groups, occ, vs, ch)
    dma = pltpu.SemaphoreType.DMA
    wide = n_vrow * n
    out = pl.pallas_call(
        functools.partial(square_kernel, dims),
        out_shape=jax.ShapeDtypeStruct((vs * ch * n_vrow * ch, vs), jnp.float32),
        in_specs=[pl.BlockSpec(memory_space=pl.ANY)] + [pl.BlockSpec(memory_space=pltpu.VMEM)] * 2,
        out_specs=pl.BlockSpec(memory_space=pltpu.VMEM),
        scratch_shapes=[
            pltpu.VMEM((1, 128), jnp.int32),
            pltpu.VMEM((occ, vs, ch, x), jnp.bfloat16),
            pltpu.VMEM((2, n_vrow, occ + 1, n, half), jnp.bfloat16),
            pltpu.VMEM((4, occ, n, half), jnp.bfloat16),
            pltpu.VMEM((groups, gw, wide), jnp.float32),
            pltpu.VMEM((2, groups, gw, wide), jnp.float32),
            pltpu.VMEM((n_vcol, groups, gw, wide), jnp.int16),
            pltpu.VMEM((n_vcol, groups, 1, wide), jnp.float32),
            pltpu.VMEM((3, groups, gw, wide), jnp.int16),
            pltpu.VMEM((3, groups, 1, wide), jnp.float32),
            pltpu.VMEM((2, groups, gw, wide), jnp.int16),
            pltpu.VMEM((2, groups, 1, wide), jnp.float32),
            pltpu.VMEM((groups, gw, wide), jnp.int16),
            pltpu.VMEM((groups, 1, wide), jnp.float32),
            pltpu.VMEM((groups, n_vrow, gw, n), jnp.int16),
            pltpu.VMEM((groups, n_vrow, 1, n), jnp.float32),
            pltpu.VMEM((n_vrow, groups, gw, n), jnp.int16),
            pltpu.VMEM((n_vrow, groups, 1, n), jnp.float32),
            pltpu.VMEM((n_vcol, 1, 128), jnp.int32),
            pltpu.VMEM((1, 1, 128), jnp.int32),
            pltpu.SMEM((n_vcol, 1, 128), jnp.int32),
            pltpu.SMEM((n_vrow, 1, 128), jnp.int32),
            dma((occ,)),
            dma((2,)),
            dma((2,)),
            dma((3, groups)),
            dma((3, groups)),
            dma((3, groups)),
            dma((3, groups)),
            dma((4,)),
            dma((4,)),
            dma((n_vcol, groups)),
            dma((3, groups)),
            dma((n_vcol, groups)),
            dma((3, groups)),
            dma((2, groups)),
            dma((groups,)),
            dma((2, groups)),
            dma((groups,)),
            dma((groups, n_vrow)),
            dma((n_vrow, groups)),
            dma((groups, n_vrow)),
            dma((n_vrow, groups)),
            pltpu.SemaphoreType.REGULAR,
        ],
        compiler_params=pltpu.CompilerParams(collective_id=0, has_side_effects=True, vmem_limit_bytes=56000000),
    )(blocks, block_ids, block_counts)
    return (out * (1.0 / (n_field * SBLK * BLOCK))).reshape(vs, ch, n_vrow, 1, ch, vs)


def solution(mesh):
    placed = (
        P(("vrow", "vcol"), "field", None, None),
        P(("vrow", "vcol"), "field", None),
        P(("vrow", "vcol"), "field"),
    )
    square = mesh.shape["field"] == 4 and mesh.shape["vcol"] == 4 and mesh.shape["vrow"] == 2
    return jax.shard_map(
        on_square_device if square else on_any_device,
        mesh=mesh,
        in_specs=placed,
        out_specs=P(("vrow", "field"), None, None, "vcol", None, None),
        check_vma=False,
    )
```
